256 devices in a mesh: dom: 128 (over x, z, y), sub: 2 (over core).
Axes of the slice: x: 4, y: 4, z: 8, core: 2. Of those that a mesh axis runs over, the one named last changes fastest.
Arguments:
- positions: float32 [3, 2097152], P(None, ('dom', 'sub')), may hold values from -6 to 6
- masses: float32 [2097152], P(('dom', 'sub')), may hold values from 0.0005 to 0.005
- old_accel: float32 [3, 2097152], P(None, ('dom', 'sub')), may hold values from -6 to 6
- active: int32 [8192], P('dom'), may hold values from 0 to 1, as said below
- parent_of: int32 [8192], P(('dom', 'sub')), may hold values from 0 to 2047
- parent_centers: float32 [3, 2048], replicated, may hold values from -4 to 4
- local_list: int32 [8192, 8], P('dom'), may hold values from 0 to 63
- near_list: int32 [8192, 8], P('dom'), may hold values from 0 to 1023, as said below
- far_list: int32 [8192, 16], P('dom'), may hold values from 0 to 2047, as said below
- send_ids: int32 [256, 128, 4], P(('dom', 'sub')), may hold values from -1 to 31, as said below
- cell_send_ids: int32 [256, 128, 8], P(('dom', 'sub')), may hold values from -1 to 31, as said below
Outputs:
- accel: float32 [3, 2097152], P(None, ('dom', 'sub'))
- parent_moments: float32 [35, 2048], P(None, 'dom')
The draws below stay inside these ranges and needn't reach their ends.
Inputs may be any that keep to these rules, and one draw needn't show every extreme that they name: On each device between 1 and 16 of its 32 groups are active, and on some device exactly 16. For device g and chip c, slots 0 to n - 1 of send_ids[g, c] name groups of device g and the others hold -1, with 1 <= n <= 4; n = 4 and n = 1 occur in every draw. For device g and chip c, slots 0 to n - 1 of cell_send_ids[g, c] name groups of device g and the others hold -1, with 1 <= n <= 8; n = 8 and n = 1 occur in every draw. `near_list`: an entry g * 4 + k names slot k of send_ids[g, c], c the chip of the row's group; that slot is never -1. `far_list`: an entry g * 8 + k names slot k of cell_send_ids[g, c], c the chip of the row's group; that slot is never -1.
All inputs are finite; a program needn't handle non-finite values.
Results may differ from the reference program's by a relative error of at most 0.0003.
Values sent between devices are 32-bit elements; how exact they have to be, the bound alone decides.
No kernel may reach another device: no remote copies, remote signals or barrier semaphores. Data moves between devices by JAX's collectives and lax.ppermute only.
A program may use at most 64 MiB of HBM per device.

```python
import math
import jax
import jax.numpy as jnp
import numpy as np
from jax import lax

BUCKET = 256
NB = 32
LOCAL_N = 8
NEAR = 8
FAR = 16
RQ = 4
RQC = 8
ACT_MAX = 16
CHIPS = 128
CORES = 256
BUCKETS = 8192
PARTICLES = 2097152
NPAR = 2048


def slot_counts(key, capacity, salt):
    count_key, spot_key = jax.random.split(jax.random.fold_in(key, salt))
    counts = jax.random.randint(count_key, (CORES, CHIPS), 1, capacity + 1)
    places = jnp.arange(CORES * CHIPS, dtype=jnp.int32).reshape(CORES, CHIPS)
    full_spot = jax.random.randint(spot_key, (), 0, CORES * CHIPS)
    thin_spot = (full_spot + CHIPS) % (CORES * CHIPS)
    counts = jnp.where(places == thin_spot, 1, counts)
    return jnp.where(places == full_spot, capacity, counts)


def send_table(key, capacity, count_salt, pick_salt):
    counts = slot_counts(key, capacity, count_salt)
    chosen = jax.random.randint(jax.random.fold_in(key, pick_salt), (CORES, CHIPS, capacity), 0, NB)
    slot_places = jnp.arange(capacity, dtype=jnp.int32)
    return jnp.where(slot_places[None, None, :] < counts[:, :, None], chosen, -1).astype(jnp.int32)


def list_table(key, capacity, count_salt, list_salt, width):
    counts = slot_counts(key, capacity, count_salt)
    source_key, slot_key = jax.random.split(jax.random.fold_in(key, list_salt))
    senders = jax.random.randint(source_key, (BUCKETS, width), 0, CORES)
    raw_slots = jax.random.randint(slot_key, (BUCKETS, width), 0, 1 << 20)
    chips = jnp.arange(BUCKETS, dtype=jnp.int32) // (BUCKETS // CHIPS)
    limits = counts[senders, chips[:, None]]
    return (senders * capacity + raw_slots % limits).astype(jnp.int32)


def draw_send_ids(key, part):
    return send_table(key, RQ, 11, 12)


def draw_near_list(key, part):
    return list_table(key, RQ, 11, 13, NEAR)


def draw_cell_send_ids(key, part):
    return send_table(key, RQC, 21, 22)


def draw_far_list(key, part):
    return list_table(key, RQC, 21, 23, FAR)


def draw_active(key, part):
    active_key = jax.random.fold_in(key, 31)
    count_key, spot_key, order_key = jax.random.split(active_key, 3)
    drawn = jax.random.randint(count_key, (CORES,), 0, ACT_MAX)
    counts = 1 + drawn * drawn // ACT_MAX
    busiest = jax.random.randint(spot_key, (), 0, CORES)
    counts = jnp.where(jnp.arange(CORES, dtype=jnp.int32) == busiest, ACT_MAX, counts)
    orders = jax.vmap(lambda order_seed: jax.random.permutation(order_seed, NB))(jax.random.split(order_key, CORES))
    return (orders < counts[:, None]).astype(jnp.int32).reshape(BUCKETS)


def draw_positions(key, part):
    center_key, offset_key = jax.random.split(jax.random.fold_in(key, 41))
    centers = jnp.clip(0.7 * jax.random.normal(center_key, (3, BUCKETS), jnp.float32), -4.0, 4.0)
    offsets = jnp.clip(0.5 * jax.random.normal(offset_key, (3, BUCKETS, BUCKET), jnp.float32), -2.0, 2.0)
    return (centers[:, :, None] + offsets).reshape(3, PARTICLES)


def plant(result, key, low, high):
    longest = result.shape.index(max(result.shape))
    spots = []
    for shift in (0, 1):
        where = [jax.random.randint(jax.random.fold_in(key, axis), (), 0, length) for axis, length in enumerate(result.shape)]
        where[longest] = (where[longest] + shift) % result.shape[longest]
        spots.append(tuple(where))
    return result.at[spots[0]].set(low).at[spots[1]].set(high)


def steps_of(key, shape, shards, least, high):
    factor_of, own = 1.0, jax.random.fold_in(key, 6)
    for dim, blocks in shards:
        steps = jnp.exp(jax.random.uniform(jax.random.fold_in(own, dim), (blocks,), jnp.float32, least / len(shards), high / len(shards)))
        factor_of = factor_of * jnp.repeat(steps, shape[dim] // blocks).reshape([-1 if axis == dim else 1 for axis in range(len(shape))])
    return factor_of


def noise(own_key, extent, spread, limit, cuts=(), kind=jnp.bfloat16):
    array = jax.random.normal(own_key, extent, jnp.float32) * spread
    if len(cuts) > 0:
        array = steps_of(own_key, extent, cuts, -0.22, 0.18) * array
    return jnp.clip(array, min=-limit, max=limit).astype(kind)


def setup_inputs(seed: int = 0) -> dict:
    arg_keys = jax.random.split(jax.random.key(seed), 12)
    return {
        "positions": draw_positions(jax.random.fold_in(arg_keys[11], 71), 0),
        "masses": jnp.clip(jnp.exp(math.log(0.005) - 2.30258502 * jax.random.uniform(arg_keys[1], (PARTICLES,), jnp.float32) ** steps_of(arg_keys[1], (PARTICLES,), ((0, 256),), -0.2, 0.2)), 0.0005, 0.005),
        "old_accel": noise(arg_keys[2], (3, PARTICLES), 1.0, 6.0, ((1, 256),), jnp.float32),
        "active": draw_active(jax.random.fold_in(arg_keys[11], 71), 0),
        "parent_of": plant(jax.random.randint(arg_keys[4], (BUCKETS,), 0, NPAR), jax.random.fold_in(arg_keys[4], 1), 0, NPAR - 1).astype(jnp.int32),
        "parent_centers": noise(arg_keys[5], (3, NPAR), 0.7, 4.0, (), jnp.float32),
        "local_list": plant(jax.random.randint(arg_keys[6], (BUCKETS, LOCAL_N), 0, 2 * NB), jax.random.fold_in(arg_keys[6], 1), 0, (2 * NB) - 1).astype(jnp.int32),
        "near_list": draw_near_list(jax.random.fold_in(arg_keys[11], 71), 0),
        "far_list": draw_far_list(jax.random.fold_in(arg_keys[11], 71), 0),
        "send_ids": draw_send_ids(jax.random.fold_in(arg_keys[11], 71), 0),
        "cell_send_ids": draw_cell_send_ids(jax.random.fold_in(arg_keys[11], 71), 0),
    }


soft_sq = 0.0025
far_sq = 0.25

def exponent_rows():
    listing = []
    for degree in range(5):
        for power_x in range(degree, -1, -1):
            for power_y in range(degree - power_x, -1, -1):
                listing.append((power_x, power_y, degree - power_x - power_y))
    return listing

def multinomial(triple):
    return math.factorial(sum(triple)) / (math.factorial(triple[0]) * math.factorial(triple[1]) * math.factorial(triple[2]))

def weight_layout():
    triples = exponent_rows()
    position = {triple: number for number, triple in enumerate(triples)}
    weight_table = np.zeros((46, 35))
    s_scale = [1.0, 1.0, 1.5, 2.5, 4.375]
    t_scale = [-0.5, -1.5, -3.75]
    mono_index = []
    radial_index = []
    for number, triple in enumerate(triples):
        weight_table[number, number] = multinomial(triple) * s_scale[sum(triple)]
        mono_index.append(number)
        radial_index.append(sum(triple))
    for number in range(10):
        triple = triples[number]
        for axis_at in range(3):
            raised = list(triple)
            raised[axis_at] += 2
            weight_table[35 + number, position[tuple(raised)]] += multinomial(triple) * t_scale[sum(triple)]
        mono_index.append(number)
        radial_index.append(sum(triple) + 1)
    for axis_one in range(3):
        for axis_two in range(3):
            raised = [0, 0, 0]
            raised[axis_one] += 2
            raised[axis_two] += 2
            weight_table[45, position[tuple(raised)]] += 0.375
    mono_index.append(0)
    radial_index.append(2)
    return (weight_table, mono_index, radial_index)

def monomial_list(comp_x, comp_y, comp_z):
    powers = []
    for component in (comp_x, comp_y, comp_z):
        series = [jnp.ones_like(component)]
        for degree in range(4):
            series.append(series[-1] * component)
        powers.append(series)
    return [powers[0][power_x] * powers[1][power_y] * powers[2][power_z] for power_x, power_y, power_z in exponent_rows()]

def moments_about(rows, centers):
    monomials = monomial_list(rows[:, 0] - centers[0][:, None], rows[:, 1] - centers[1][:, None], rows[:, 2] - centers[2][:, None])
    return jnp.stack([lax.optimization_barrier(jnp.sum(rows[:, 3] * monomial, axis=1)) for monomial in monomials])

def bucket_cells(rows):
    centers = lax.optimization_barrier(jnp.mean(rows[:, :3], axis=2)).T
    moments = moments_about(rows, centers)
    return jnp.concatenate([moments.T, centers.T], axis=1)

def near_field(targets, sources):

    def add_source(number, running):
        source = lax.dynamic_index_in_dim(sources, number, 0, keepdims=False)
        offset = source[:3, :, None] - targets[:, None, :]
        dist_sq = lax.optimization_barrier(jnp.sum(offset * offset, axis=0)) + soft_sq
        weight = source[3][:, None] / (dist_sq * jnp.sqrt(dist_sq))
        return running + lax.optimization_barrier(jnp.sum(offset * weight[None], axis=1))
    return lax.fori_loop(0, sources.shape[0], add_source, jnp.zeros(targets.shape, jnp.float32))

def far_field(targets, cells):
    weight_table, mono_index, radial_index = weight_layout()
    centers = cells[:, 35:38].T
    weights = jnp.dot(cells[:, :35], jnp.asarray(weight_table.T, dtype=jnp.float32), precision=lax.Precision.HIGHEST)

    def potential(points):
        offset = points[:, None, :] - centers[:, :, None]
        rho_sq = lax.optimization_barrier(jnp.sum(offset * offset, axis=0)) + far_sq
        inv_rho = 1.0 / jnp.sqrt(rho_sq)
        inv_sq = 1.0 / rho_sq
        radial = [inv_rho]
        for degree in range(4):
            radial.append(radial[-1] * inv_sq)
        monomials = monomial_list(offset[0], offset[1], offset[2])
        running = jnp.zeros(rho_sq.shape, jnp.float32)
        for number in range(46):
            running = running + monomials[mono_index[number]] * weights[:, number][:, None] * radial[radial_index[number]]
        return jnp.sum(running)
    return jax.grad(potential)(targets)

def reference(positions, masses, old_accel, active, parent_of, parent_centers, local_list, near_list, far_list, send_ids, cell_send_ids):
    rows = jnp.concatenate([positions, masses[None]], axis=0).reshape(4, BUCKETS, BUCKET).transpose(1, 0, 2)
    cells = bucket_cells(rows)
    parent_terms = moments_about(rows, parent_centers[:, parent_of])
    parent_moments = jax.ops.segment_sum(parent_terms.T, parent_of, num_segments=NPAR).T
    per_chip = BUCKETS // CHIPS
    bucket_ids = jnp.arange(BUCKETS, dtype=jnp.int32)
    chip_of = bucket_ids // per_chip
    local_global = (chip_of * per_chip)[:, None] + local_list
    near_device = near_list // RQ
    near_global = near_device * NB + send_ids[near_device, chip_of[:, None], near_list % RQ]
    far_device = far_list // RQC
    far_global = far_device * NB + cell_send_ids[far_device, chip_of[:, None], far_list % RQC]
    source_ids = jnp.concatenate([local_global, near_global], axis=1)

    def one_bucket(bucket_at):

        def compute(bucket_row):
            targets = rows[bucket_row, :3]
            return near_field(targets, rows[source_ids[bucket_row]]) + far_field(targets, cells[far_global[bucket_row]])

        def skipped(bucket_row):
            return jnp.zeros((3, BUCKET), jnp.float32)
        return lax.cond(active[bucket_at] > 0, compute, skipped, bucket_at)
    computed = lax.map(one_bucket, bucket_ids)
    new_accel = computed.transpose(1, 0, 2).reshape(3, PARTICLES)
    active_cols = jnp.repeat(active > 0, BUCKET)
    return (jnp.where(active_cols[None, :], new_accel, old_accel), parent_moments)
```

```python
import jax
import jax.numpy as jnp
from jax import lax
from jax.experimental import pallas as pl
from jax.experimental.pallas import tpu as pltpu
from jax.sharding import PartitionSpec as P

BUCKET = 256
NB = 32
RQ = 4
RQC = 8
SHARE = NB // 2 + RQC
SOFT_SQ = 0.0025
FAR_SQ = 0.25
F32 = jnp.float32
SMEM = pl.BlockSpec(memory_space=pltpu.SMEM)
VMEM = pl.BlockSpec(memory_space=pltpu.VMEM)


def exponent_rows():
    listing = []
    for degree in range(5):
        for power_x in range(degree, -1, -1):
            for power_y in range(degree - power_x, -1, -1):
                listing.append((power_x, power_y, degree - power_x - power_y))
    return listing


TRIPLES = exponent_rows()
SPOT = {triple: number for number, triple in enumerate(TRIPLES)}
AXES = ((1, 0, 0), (0, 1, 0), (0, 0, 1))


def plus(*triples):
    return tuple(sum(parts) for parts in zip(*triples))


def lanes_of(ref, comp, b):
    return ref[comp : comp + 1, pl.ds(pl.multiple_of(b * BUCKET, BUCKET), BUCKET)]


def pack_kernel(ids_ref, pos_ref, mass_ref, rows_ref, tiles_ref, blocks_ref, flat):
    for b in range(NB):
        at = pl.ds(b * BUCKET, BUCKET)
        for comp in range(3):
            rows_ref[comp, b : b + 1, :] = pos_ref[comp : comp + 1, at]
        rows_ref[3, b : b + 1, :] = mass_ref[0:1, at]
    quarter = lax.broadcasted_iota(jnp.int32, (NB, 128), 1) // 32
    for s in range(8):
        tile = None
        for comp in range(4):
            part = rows_ref[comp, :, (s // 4) * 128 : (s // 4) * 128 + 128]
            shift = (comp - s % 4) * 32 % 128
            if shift:
                part = pltpu.roll(part, shift, 1)
            tile = part if tile is None else jnp.where(quarter == comp, part, tile)
        flat[pl.ds(s, NB, stride=8), :] = tile
    for b in range(NB):
        tiles_ref[b] = flat[8 * b : 8 * b + 8, :]

    def fill(step, carry):
        for part in range(4):
            dest = step * 4 + part
            for slot in range(RQ):
                group = jnp.maximum(ids_ref[slot, dest], 0)
                blocks_ref[dest, slot] = tiles_ref[group]
        return carry

    lax.fori_loop(0, blocks_ref.shape[0] // 4, fill, 0)


def monomial_sums(offsets, mass):
    x, y, z = offsets
    known = {(0, 0, 0): mass}
    sums = []
    for triple in TRIPLES:
        if triple not in known:
            axis = next(a for a in range(3) if triple[a] > 0)
            lower = tuple(p - (1 if a == axis else 0) for a, p in enumerate(triple))
            known[triple] = known[lower] * offsets[axis]
        sums.append(jnp.sum(known[triple], axis=1, keepdims=True))
    return sums


def cell_columns(moments, center):
    m = {triple: moments[number] for number, triple in enumerate(TRIPLES)}
    trace1 = [sum(m[plus(e, f, f)] for f in AXES) for e in AXES]
    pairs = [t for t in TRIPLES if sum(t) == 2]
    trace2 = [sum(m[plus(t, f, f)] for f in AXES) for t in pairs]
    full = trace2[0] + trace2[3] + trace2[5]
    scale = (1.0, 1.0, 1.5, 2.5, 4.375)
    columns = [m[t] * scale[sum(t)] for t in TRIPLES]
    columns += center
    columns += [-0.5 * (m[(2, 0, 0)] + m[(0, 2, 0)] + m[(0, 0, 2)])]
    columns += [1.5 * t for t in trace1]
    columns += [3.75 * t for t in trace2]
    columns += [0.375 * full]
    return columns


def spread(columns, lane):
    table = jnp.zeros(lane.shape, F32)
    for number, column in enumerate(columns):
        table = jnp.where(lane == number, column, table)
    return table


def moment_kernel(
    parent_ref, pcent_ref, rows_ref, slots_ref, cells_ref, contrib_ref, about, terms
):
    lane = lax.broadcasted_iota(jnp.int32, (NB, 128), 1)
    for b in range(NB):
        parent = parent_ref[b]
        for comp in range(3):
            about[comp, b : b + 1, :] = jnp.full((1, 128), pcent_ref[comp, parent], F32)
    mass = rows_ref[3]
    coords = [rows_ref[comp] for comp in range(3)]
    centers = [jnp.sum(c, axis=1, keepdims=True) * (1.0 / BUCKET) for c in coords]
    sums = monomial_sums([c - o for c, o in zip(coords, centers)], mass)
    table = spread(cell_columns(sums, centers), lane)
    half = NB // 2
    cells_ref[half:, : slots_ref.shape[1]] = slots_ref[...].astype(F32)
    cells_ref[:half, :] = jnp.where(lane[:half] < 64, table[:half], pltpu.roll(table[half:], 64, 1))
    parents = [about[comp, :, 0:1] for comp in range(3)]
    sums = monomial_sums([c - o for c, o in zip(coords, parents)], mass)
    terms[0] = spread(sums, lane)
    terms[1] = pltpu.roll(terms[0], 64, 1)
    contrib_ref[...] = jnp.zeros(contrib_ref.shape, F32)
    for b in range(NB):
        parent = parent_ref[b]
        row = pl.ds((parent // 16) * 8 + parent % 8, 1)
        contrib_ref[row, :] = contrib_ref[row, :] + terms[(parent % 16) // 8, b : b + 1, :]


def near_body(tiles_at, targets):
    tx, ty, tz = targets

    def add_group(number, sums):
        tile = tiles_at(number)
        ax, ay, az = sums
        for g in range(32):
            dx = tile[:, g : g + 1] - tx
            dy = tile[:, 32 + g : 33 + g] - ty
            dz = tile[:, 64 + g : 65 + g] - tz
            inv = lax.rsqrt(dx * dx + dy * dy + (dz * dz + SOFT_SQ))
            weight = tile[:, 96 + g : 97 + g] * inv * (inv * inv)
            ax = ax + weight * dx
            ay = ay + weight * dy
            az = az + weight * dz
        return ax, ay, az

    return add_group


def each_active(sub, act_ref, visit):
    def step(t, carry):
        half = t // NB
        b = t % NB
        row = jnp.where(half == 0, sub, 1 - sub) * NB + b

        @pl.when(act_ref[row] > 0)
        def _():
            visit(half, b, row)

        return carry

    lax.fori_loop(0, 2 * NB, step, 0)


def load_targets(targets, half, b):
    return [
        jnp.broadcast_to(lanes_of(targets.at[half], comp, b), (8, BUCKET)) for comp in range(3)
    ]


def add_rows(ref, half, b, values):
    at = pl.ds(pl.multiple_of(b * BUCKET, BUCKET), BUCKET)
    for comp in range(3):
        row = jnp.sum(values[comp], axis=0, keepdims=True)
        ref[half, comp : comp + 1, at] = ref[half, comp : comp + 1, at] + row


def local_kernel(sub_ref, act_ref, list_ref, pos_ref, other_ref, tiles_ref, out_ref, targets, names):
    sub = sub_ref[0]
    targets[0] = pos_ref[...]
    targets[1] = other_ref[...]
    out_ref[...] = jnp.zeros(out_ref.shape, F32)

    def visit(half, b, row):
        count = 0
        for k in range(8):
            entry = list_ref[k, row]
            names[count] = entry % NB
            count = count + jnp.where(entry // NB == sub, 1, 0)
        body = near_body(lambda n: tiles_ref[names[n]], load_targets(targets, half, b))
        zero = jnp.zeros((8, BUCKET), F32)
        add_rows(out_ref, half, b, lax.fori_loop(0, count, body, (zero, zero, zero)))

    each_active(sub, act_ref, visit)


def remote_kernel(
    sub_ref, act_ref, list_ref, pos_ref, other_ref, pool_ref, part_ref, out_ref, targets, names
):
    sub = sub_ref[0]
    targets[0] = pos_ref[...]
    targets[1] = other_ref[...]
    out_ref[...] = part_ref[...]

    def visit(half, b, row):
        count = 0
        for k in range(8):
            entry = list_ref[k, row]
            names[count] = (entry // (2 * RQ)) * RQ + entry % RQ
            count = count + jnp.where((entry // RQ) % 2 == sub, 1, 0)
        body = near_body(lambda n: pool_ref[names[n]], load_targets(targets, half, b))
        zero = jnp.zeros((8, BUCKET), F32)
        add_rows(out_ref, half, b, lax.fori_loop(0, count, body, (zero, zero, zero)))

    each_active(sub, act_ref, visit)


def contract(tensor, axis, weighted):
    total = None
    for triple, value in weighted.items():
        term = tensor[plus(triple, AXES[axis])] * value
        total = term if total is None else total + term
    return total


def cell_pull(table, targets):
    def column(number):
        return table[:, number : number + 1]

    m = {triple: column(number) for number, triple in enumerate(TRIPLES)}
    r = [targets[a] - column(35 + a) for a in range(3)]
    x, y, z = r
    rho_sq = x * x + y * y + (z * z + FAR_SQ)
    inv = lax.rsqrt(rho_sq)
    inv_sq = inv * inv
    u = [inv]
    for _ in range(5):
        u.append(u[-1] * inv_sq)
    xx, yy, zz, xy, xz, yz = x * x, y * y, z * z, x * y, x * z, y * z
    first = {(1, 0, 0): x, (0, 1, 0): y, (0, 0, 1): z}
    second = {
        (2, 0, 0): xx,
        (1, 1, 0): 2.0 * xy,
        (1, 0, 1): 2.0 * xz,
        (0, 2, 0): yy,
        (0, 1, 1): 2.0 * yz,
        (0, 0, 2): zz,
    }
    x3, y3, z3 = 3.0 * x, 3.0 * y, 3.0 * z
    third = {
        (3, 0, 0): xx * x,
        (2, 1, 0): xx * y3,
        (2, 0, 1): xx * z3,
        (1, 2, 0): yy * x3,
        (1, 1, 1): xy * (2.0 * z3),
        (1, 0, 2): zz * x3,
        (0, 3, 0): yy * y,
        (0, 2, 1): yy * z3,
        (0, 1, 2): zz * y3,
        (0, 0, 3): zz * z,
    }
    pairs = [t for t in TRIPLES if sum(t) == 2]
    trace2 = {t: column(42 + number) for number, t in enumerate(pairs)}
    grad = []
    q1, q2, q3, q4 = column(38), column(48), None, None
    for a in range(3):
        m1 = m[AXES[a]]
        a2 = contract(m, a, first)
        b2 = column(39 + a)
        a3 = contract(m, a, second)
        b3 = contract(trace2, a, first)
        a4 = contract(m, a, third)
        grad.append(
            m1 * u[1]
            + (a2 + (a2 - b2)) * u[2]
            + (a3 + 2.0 * (a3 - b3)) * u[3]
            + (4.0 * a4) * u[4]
        )
        q1 = q1 + r[a] * m1
        q2 = q2 + r[a] * (a2 - b2)
        low, high = r[a] * (a3 - b3), r[a] * a4
        q3 = low if q3 is None else q3 + low
        q4 = high if q4 is None else q4 + high
    pull = (
        m[(0, 0, 0)] * u[1] + 3.0 * q1 * u[2] + 5.0 * q2 * u[3] + 7.0 * q3 * u[4] + 9.0 * q4 * u[5]
    )
    return [grad[a] - r[a] * pull for a in range(3)]


def far_kernel(
    sub_ref,
    act_ref,
    list_ref,
    ids_ref,
    pos_ref,
    other_ref,
    cells_ref,
    part_ref,
    out_ref,
    targets,
    picked,
):
    sub = sub_ref[0]
    targets[0] = pos_ref[...]
    targets[1] = other_ref[...]
    out_ref[...] = part_ref[...]
    half_rows = NB // 2

    def visit(half, b, row):
        picked[...] = jnp.zeros(picked.shape, F32)
        count = 0
        for k in range(16):
            entry = list_ref[k, row]
            device = entry // (2 * RQC)
            group = jnp.maximum(ids_ref[device * RQC + entry % RQC], 0)
            cell = cells_ref[pl.ds(device * SHARE + group % half_rows, 1), :]
            mine = (entry // RQC) % 2 == sub
            cell = jnp.where(group >= half_rows, pltpu.roll(cell, 64, 1), cell)
            picked[pl.ds(count, 1), :] = jnp.where(mine, cell, 0.0)
            count = count + jnp.where(mine, 1, 0)
        sides = load_targets(targets, half, b)

        def add_cells(step, sums):
            table = picked[pl.ds(pl.multiple_of(step * 8, 8), 8), :]
            return tuple(s + p for s, p in zip(sums, cell_pull(table, sides)))

        zero = jnp.zeros((8, BUCKET), F32)
        sums = lax.fori_loop(0, (count + 7) // 8, add_cells, (zero, zero, zero))
        add_rows(out_ref, half, b, sums)

    each_active(sub, act_ref, visit)


def finish_kernel(
    sub_ref, act_ref, part_ref, came_ref, old_ref, mom_ref, mom_came_ref, accel_ref, parent_ref
):
    sub = sub_ref[0]
    for b in range(NB):
        at = pl.ds(b * BUCKET, BUCKET)
        live = act_ref[sub * NB + b] > 0
        accel_ref[:, at] = jnp.where(live, part_ref[0, :, at] + came_ref[:, at], old_ref[:, at])
    both = (mom_ref[...] + mom_came_ref[...]).T
    parent_ref[:, 0:8] = both[0:35]
    parent_ref[:, 8:16] = both[64:99]


def shape(*dims):
    return jax.ShapeDtypeStruct(dims, F32)


def local(
    positions,
    masses,
    old_accel,
    active,
    parent_of,
    parent_centers,
    local_list,
    near_list,
    far_list,
    send_ids,
    cell_send_ids,
):
    chips = lax.axis_size("dom")
    own = NB * BUCKET
    me = lax.axis_index("sub").astype(jnp.int32).reshape(1)
    swap = [(0, 1), (1, 0)]
    target_scratch = pltpu.VMEM((2, 3, own), F32)
    params = pltpu.CompilerParams(vmem_limit_bytes=32 << 20)

    other = lax.ppermute(positions, "sub", swap)
    slot_ids = cell_send_ids.transpose(0, 2, 1).reshape(RQC, chips)

    rows, tiles, blocks = pl.pallas_call(
        pack_kernel,
        in_specs=[SMEM, VMEM, VMEM],
        out_specs=[VMEM, VMEM, VMEM],
        out_shape=[shape(4, NB, BUCKET), shape(NB, 8, 128), shape(chips, RQ, 8, 128)],
        scratch_shapes=[pltpu.VMEM((NB * 8, 128), F32)],
        compiler_params=params,
        name="pack",
    )(send_ids[0].T, positions, masses.reshape(1, own))
    pool = lax.all_to_all(
        blocks.reshape(chips, RQ * 8, 128), "dom", split_axis=0, concat_axis=0, tiled=True
    ).reshape(chips * RQ, 8, 128)

    cells, contrib = pl.pallas_call(
        moment_kernel,
        in_specs=[SMEM, SMEM, VMEM, VMEM],
        out_specs=[VMEM, VMEM],
        out_shape=[shape(SHARE, 128), shape(chips * 8, 128)],
        scratch_shapes=[pltpu.VMEM((3, NB, 128), F32), pltpu.VMEM((2, NB, 128), F32)],
        compiler_params=params,
        name="moments",
    )(parent_of, parent_centers, rows, slot_ids)
    cell_pool = lax.all_gather(cells, "dom", axis=0, tiled=True)
    owned = lax.psum_scatter(contrib, "dom", scatter_dimension=0, tiled=True)

    part = pl.pallas_call(
        local_kernel,
        in_specs=[SMEM, SMEM, SMEM, VMEM, VMEM, VMEM],
        out_specs=VMEM,
        out_shape=shape(2, 3, own),
        scratch_shapes=[target_scratch, pltpu.SMEM((9,), jnp.int32)],
        compiler_params=params,
        cost_estimate=pl.CostEstimate(flops=2 << 30, transcendentals=1 << 27, bytes_accessed=1 << 20),
        name="near_local",
    )(me, active, local_list.T, positions, other, tiles)

    all_ids = cell_pool.reshape(chips, SHARE, 128)[:, NB // 2 :]
    my_ids = lax.dynamic_index_in_dim(all_ids, lax.axis_index("dom"), 2, keepdims=False)
    my_ids = my_ids.astype(jnp.int32).reshape(chips * RQC)
    part = pl.pallas_call(
        far_kernel,
        in_specs=[SMEM, SMEM, SMEM, SMEM, VMEM, VMEM, VMEM, VMEM],
        out_specs=VMEM,
        out_shape=shape(2, 3, own),
        scratch_shapes=[target_scratch, pltpu.VMEM((24, 128), F32)],
        compiler_params=params,
        cost_estimate=pl.CostEstimate(flops=1 << 28, transcendentals=1 << 22, bytes_accessed=1 << 20),
        name="far",
    )(me, active, far_list.T, my_ids, positions, other, cell_pool, part)

    part = pl.pallas_call(
        remote_kernel,
        in_specs=[SMEM, SMEM, SMEM, VMEM, VMEM, VMEM, VMEM],
        out_specs=VMEM,
        out_shape=shape(2, 3, own),
        scratch_shapes=[target_scratch, pltpu.SMEM((9,), jnp.int32)],
        compiler_params=params,
        cost_estimate=pl.CostEstimate(flops=2 << 30, transcendentals=1 << 27, bytes_accessed=1 << 20),
        name="near_remote",
    )(me, active, near_list.T, positions, other, pool, part)

    came = lax.ppermute(part[1], "sub", swap)
    owned_came = lax.ppermute(owned, "sub", swap)
    accel, parents = pl.pallas_call(
        finish_kernel,
        in_specs=[SMEM, SMEM, VMEM, VMEM, VMEM, VMEM, VMEM],
        out_specs=[VMEM, VMEM],
        out_shape=[shape(3, own), shape(35, 16)],
        compiler_params=params,
        name="finish",
    )(me, active, part, came, old_accel, owned, owned_came)
    return accel, parents


def solution(mesh):
    both = ("dom", "sub")
    in_specs = (
        P(None, both),
        P(both),
        P(None, both),
        P("dom"),
        P(both),
        P(),
        P("dom", None),
        P("dom", None),
        P("dom", None),
        P(both, None, None),
        P(both, None, None),
    )
    out_specs = (P(None, both), P(None, "dom"))
    return jax.shard_map(local, mesh=mesh, in_specs=in_specs, out_specs=out_specs, check_vma=False)
```

```python
import functools

import jax
import jax.numpy as jnp
from jax import lax
from jax.experimental import pallas as pl
from jax.experimental.pallas import tpu as pltpu
from jax.sharding import PartitionSpec as P

BUCKET = 256
NB = 32
RQ = 4
RQC = 8
CELL_LANE = 70
SOFT_SQ = 0.0025
FAR_SQ = 0.25
F32 = jnp.float32
SMEM = pl.BlockSpec(memory_space=pltpu.SMEM)
VMEM = pl.BlockSpec(memory_space=pltpu.VMEM)


def exponent_rows():
    listing = []
    for degree in range(5):
        for power_x in range(degree, -1, -1):
            for power_y in range(degree - power_x, -1, -1):
                listing.append((power_x, power_y, degree - power_x - power_y))
    return listing


TRIPLES = exponent_rows()
SPOT = {triple: number for number, triple in enumerate(TRIPLES)}
AXES = ((1, 0, 0), (0, 1, 0), (0, 0, 1))


def plus(*triples):
    return tuple(sum(parts) for parts in zip(*triples))


def lanes_of(ref, comp, b):
    return ref[comp : comp + 1, pl.ds(pl.multiple_of(b * BUCKET, BUCKET), BUCKET)]


def monomial_sums(offsets, mass):
    x, y, z = offsets
    known = {(0, 0, 0): mass}
    sums = []
    for triple in TRIPLES:
        if triple not in known:
            axis = next(a for a in range(3) if triple[a] > 0)
            lower = tuple(p - (1 if a == axis else 0) for a, p in enumerate(triple))
            known[triple] = known[lower] * offsets[axis]
        sums.append(jnp.sum(known[triple], axis=1, keepdims=True))
    return sums


def cell_columns(moments, center):
    m = {triple: moments[number] for number, triple in enumerate(TRIPLES)}
    trace1 = [sum(m[plus(e, f, f)] for f in AXES) for e in AXES]
    pairs = [t for t in TRIPLES if sum(t) == 2]
    trace2 = [sum(m[plus(t, f, f)] for f in AXES) for t in pairs]
    full = trace2[0] + trace2[3] + trace2[5]
    scale = (1.0, 1.0, 1.5, 2.5, 4.375)
    columns = [m[t] * scale[sum(t)] for t in TRIPLES]
    columns += center
    columns += [-0.5 * (m[(2, 0, 0)] + m[(0, 2, 0)] + m[(0, 0, 2)])]
    columns += [1.5 * t for t in trace1]
    columns += [3.75 * t for t in trace2]
    columns += [0.375 * full]
    return columns


def spread(columns, lane):
    table = jnp.zeros(lane.shape, F32)
    for number, column in enumerate(columns):
        table = jnp.where(lane == number, column, table)
    return table


def pack_kernel(
    ids_ref,
    cell_ids_ref,
    parent_ref,
    pcent_ref,
    pos_ref,
    mass_ref,
    tiles_ref,
    first_ref,
    second_ref,
    rows,
    flat,
    about,
    terms,
    cells,
    contrib,
):
    chips = first_ref.shape[0]
    for b in range(NB):
        at = pl.ds(b * BUCKET, BUCKET)
        for comp in range(3):
            rows[comp, b : b + 1, :] = pos_ref[comp : comp + 1, at]
        rows[3, b : b + 1, :] = mass_ref[0:1, at]
        parent = parent_ref[b]
        for comp in range(3):
            about[comp, b : b + 1, :] = jnp.full((1, 128), pcent_ref[comp, parent], F32)
    lane = lax.broadcasted_iota(jnp.int32, (NB, 128), 1)
    for s in range(8):
        tile = None
        for comp in range(4):
            part = rows[comp, :, (s // 4) * 128 : (s // 4) * 128 + 128]
            shift = (comp - s % 4) * 32 % 128
            if shift:
                part = pltpu.roll(part, shift, 1)
            tile = part if tile is None else jnp.where(lane // 32 == comp, part, tile)
        flat[pl.ds(s, NB, stride=8), :] = tile
    for b in range(NB):
        tiles_ref[b] = flat[8 * b : 8 * b + 8, :]

    coords = [rows[comp] for comp in range(3)]
    centers = [jnp.sum(c, axis=1, keepdims=True) * (1.0 / BUCKET) for c in coords]
    sums = monomial_sums([c - o for c, o in zip(coords, centers)], rows[3])
    cells[...] = spread(cell_columns(sums, centers), lane - CELL_LANE)
    parents = [about[comp, :, 0:1] for comp in range(3)]
    sums = monomial_sums([c - o for c, o in zip(coords, parents)], rows[3])
    terms[0] = spread(sums, lane)
    terms[1] = pltpu.roll(terms[0], 35, 1)
    contrib[...] = jnp.zeros(contrib.shape, F32)
    for b in range(NB):
        parent = parent_ref[b]
        row = pl.ds((parent // 16) * 8 + parent % 8, 1)
        contrib[row, :] = contrib[row, :] + terms[(parent % 16) // 8, b : b + 1, :]

    def fill(step, carry):
        for part in range(2):
            dest = step * 2 + part
            for slot in range(RQ):
                tile = tiles_ref[jnp.maximum(ids_ref[slot, dest], 0)]
                if slot < 2:
                    first_ref[dest, slot] = tile
                else:
                    second_ref[dest, slot - 2] = tile
            for slot in range(RQC):
                cell = cells[pl.ds(jnp.maximum(cell_ids_ref[slot, dest], 0), 1), :]
                first_ref[dest, 2, slot : slot + 1, :] = cell
            own = contrib[pl.ds(pl.multiple_of(dest * 8, 8), 8), :]
            first_ref[dest, 2] = first_ref[dest, 2] + own
        return carry

    lax.fori_loop(0, chips // 2, fill, 0)


def near_body(tiles_at, targets):
    tx, ty, tz = targets

    def add_group(number, sums):
        tile = tiles_at(number)
        ax, ay, az = sums
        for g in range(32):
            dx = tile[:, g : g + 1] - tx
            dy = tile[:, 32 + g : 33 + g] - ty
            dz = tile[:, 64 + g : 65 + g] - tz
            inv = lax.rsqrt(dx * dx + dy * dy + (dz * dz + SOFT_SQ))
            weight = tile[:, 96 + g : 97 + g] * inv * (inv * inv)
            ax = ax + weight * dx
            ay = ay + weight * dy
            az = az + weight * dz
        return ax, ay, az

    return add_group


def each_active(sub, act_ref, visit):
    def step(t, carry):
        half = t // NB
        b = t % NB
        row = jnp.where(half == 0, sub, 1 - sub) * NB + b

        @pl.when(act_ref[row] > 0)
        def _():
            visit(half, b, row)

        return carry

    lax.fori_loop(0, 2 * NB, step, 0)


def load_targets(targets, half, b):
    return [
        jnp.broadcast_to(lanes_of(targets.at[half], comp, b), (8, BUCKET)) for comp in range(3)
    ]


def add_rows(ref, half, b, values):
    at = pl.ds(pl.multiple_of(b * BUCKET, BUCKET), BUCKET)
    for comp in range(3):
        row = jnp.sum(values[comp], axis=0, keepdims=True)
        ref[half, comp : comp + 1, at] = ref[half, comp : comp + 1, at] + row


def local_kernel(sub_ref, act_ref, list_ref, pos_ref, other_ref, tiles_ref, out_ref, targets, names):
    sub = sub_ref[0]
    targets[0] = pos_ref[...]
    targets[1] = other_ref[...]
    out_ref[...] = jnp.zeros(out_ref.shape, F32)

    def visit(half, b, row):
        count = 0
        for k in range(8):
            entry = list_ref[k, row]
            names[count] = entry % NB
            count = count + jnp.where(entry // NB == sub, 1, 0)
        body = near_body(lambda n: tiles_ref[names[n]], load_targets(targets, half, b))
        zero = jnp.zeros((8, BUCKET), F32)
        add_rows(out_ref, half, b, lax.fori_loop(0, count, body, (zero, zero, zero)))

    each_active(sub, act_ref, visit)


def remote_kernel(base, width, stride, *refs):
    sub_ref, act_ref, list_ref, pos_ref, other_ref, pool_ref, part_ref, out_ref, targets, names = refs
    sub = sub_ref[0]
    targets[0] = pos_ref[...]
    targets[1] = other_ref[...]
    out_ref[...] = part_ref[...]

    def visit(half, b, row):
        count = 0
        for k in range(8):
            entry = list_ref[k, row]
            slot = entry % RQ - base
            names[count] = (entry // (2 * RQ)) * stride + slot
            mine = ((entry // RQ) % 2 == sub) & (slot >= 0) & (slot < width)
            count = count + jnp.where(mine, 1, 0)

        @pl.when(count > 0)
        def _():
            body = near_body(lambda n: pool_ref[names[n]], load_targets(targets, half, b))
            zero = jnp.zeros((8, BUCKET), F32)
            add_rows(out_ref, half, b, lax.fori_loop(0, count, body, (zero, zero, zero)))

    each_active(sub, act_ref, visit)


def contract(tensor, axis, weighted):
    total = None
    for triple, value in weighted.items():
        term = tensor[plus(triple, AXES[axis])] * value
        total = term if total is None else total + term
    return total


def cell_pull(table, targets):
    def column(number):
        return table[:, CELL_LANE + number : CELL_LANE + number + 1]

    m = {triple: column(number) for number, triple in enumerate(TRIPLES)}
    r = [targets[a] - column(35 + a) for a in range(3)]
    x, y, z = r
    rho_sq = x * x + y * y + (z * z + FAR_SQ)
    inv = lax.rsqrt(rho_sq)
    inv_sq = inv * inv
    u = [inv]
    for _ in range(5):
        u.append(u[-1] * inv_sq)
    xx, yy, zz, xy, xz, yz = x * x, y * y, z * z, x * y, x * z, y * z
    first = {(1, 0, 0): x, (0, 1, 0): y, (0, 0, 1): z}
    second = {
        (2, 0, 0): xx,
        (1, 1, 0): 2.0 * xy,
        (1, 0, 1): 2.0 * xz,
        (0, 2, 0): yy,
        (0, 1, 1): 2.0 * yz,
        (0, 0, 2): zz,
    }
    x3, y3, z3 = 3.0 * x, 3.0 * y, 3.0 * z
    third = {
        (3, 0, 0): xx * x,
        (2, 1, 0): xx * y3,
        (2, 0, 1): xx * z3,
        (1, 2, 0): yy * x3,
        (1, 1, 1): xy * (2.0 * z3),
        (1, 0, 2): zz * x3,
        (0, 3, 0): yy * y,
        (0, 2, 1): yy * z3,
        (0, 1, 2): zz * y3,
        (0, 0, 3): zz * z,
    }
    pairs = [t for t in TRIPLES if sum(t) == 2]
    trace2 = {t: column(42 + number) for number, t in enumerate(pairs)}
    grad = []
    q1, q2, q3, q4 = column(38), column(48), None, None
    for a in range(3):
        m1 = m[AXES[a]]
        a2 = contract(m, a, first)
        b2 = column(39 + a)
        a3 = contract(m, a, second)
        b3 = contract(trace2, a, first)
        a4 = contract(m, a, third)
        grad.append(
            m1 * u[1]
            + (a2 + (a2 - b2)) * u[2]
            + (a3 + 2.0 * (a3 - b3)) * u[3]
            + (4.0 * a4) * u[4]
        )
        q1 = q1 + r[a] * m1
        q2 = q2 + r[a] * (a2 - b2)
        low, high = r[a] * (a3 - b3), r[a] * a4
        q3 = low if q3 is None else q3 + low
        q4 = high if q4 is None else q4 + high
    pull = (
        m[(0, 0, 0)] * u[1] + 3.0 * q1 * u[2] + 5.0 * q2 * u[3] + 7.0 * q3 * u[4] + 9.0 * q4 * u[5]
    )
    return [grad[a] - r[a] * pull for a in range(3)]


def far_kernel(
    sub_ref,
    act_ref,
    list_ref,
    pos_ref,
    other_ref,
    pool_ref,
    part_ref,
    out_ref,
    owned_ref,
    targets,
    picked,
):
    sub = sub_ref[0]
    targets[0] = pos_ref[...]
    targets[1] = other_ref[...]
    out_ref[...] = part_ref[...]

    def gather_owned(step, total):
        for part in range(2):
            total = total + pool_ref[step * 2 + part, 2]
        return total

    chips = pool_ref.shape[0]
    owned_ref[...] = lax.fori_loop(0, chips // 2, gather_owned, jnp.zeros((8, 128), F32))

    def visit(half, b, row):
        picked[...] = jnp.zeros(picked.shape, F32)
        count = 0
        for k in range(16):
            entry = list_ref[k, row]
            cell = pool_ref[entry // (2 * RQC), 2, pl.ds(entry % RQC, 1), :]
            mine = (entry // RQC) % 2 == sub
            picked[pl.ds(count, 1), :] = jnp.where(mine, cell, 0.0)
            count = count + jnp.where(mine, 1, 0)
        sides = load_targets(targets, half, b)

        def add_cells(step, sums):
            table = picked[pl.ds(pl.multiple_of(step * 8, 8), 8), :]
            return tuple(s + p for s, p in zip(sums, cell_pull(table, sides)))

        zero = jnp.zeros((8, BUCKET), F32)
        sums = lax.fori_loop(0, (count + 7) // 8, add_cells, (zero, zero, zero))
        add_rows(out_ref, half, b, sums)

    each_active(sub, act_ref, visit)


def finish_kernel(
    sub_ref, act_ref, part_ref, came_ref, old_ref, mom_ref, mom_came_ref, accel_ref, parent_ref
):
    sub = sub_ref[0]
    for b in range(NB):
        at = pl.ds(b * BUCKET, BUCKET)
        live = act_ref[sub * NB + b] > 0
        accel_ref[:, at] = jnp.where(live, part_ref[0, :, at] + came_ref[:, at], old_ref[:, at])
    both = (mom_ref[...] + mom_came_ref[...]).T
    parent_ref[:, 0:8] = both[0:35]
    parent_ref[:, 8:16] = both[35:70]


def shape(*dims):
    return jax.ShapeDtypeStruct(dims, F32)


def local(
    positions,
    masses,
    old_accel,
    active,
    parent_of,
    parent_centers,
    local_list,
    near_list,
    far_list,
    send_ids,
    cell_send_ids,
):
    chips = lax.axis_size("dom")
    own = NB * BUCKET
    me = lax.axis_index("sub").astype(jnp.int32).reshape(1)
    swap = [(0, 1), (1, 0)]
    target_scratch = pltpu.VMEM((2, 3, own), F32)
    name_scratch = pltpu.SMEM((9,), jnp.int32)
    params = pltpu.CompilerParams(vmem_limit_bytes=32 << 20)

    other = lax.ppermute(positions, "sub", swap)

    tiles, first, second = pl.pallas_call(
        pack_kernel,
        in_specs=[SMEM, SMEM, SMEM, SMEM, VMEM, VMEM],
        out_specs=[VMEM, VMEM, VMEM],
        out_shape=[shape(NB, 8, 128), shape(chips, 3, 8, 128), shape(chips, 2, 8, 128)],
        scratch_shapes=[
            pltpu.VMEM((4, NB, BUCKET), F32),
            pltpu.VMEM((NB * 8, 128), F32),
            pltpu.VMEM((3, NB, 128), F32),
            pltpu.VMEM((2, NB, 128), F32),
            pltpu.VMEM((NB, 128), F32),
            pltpu.VMEM((chips * 8, 128), F32),
        ],
        compiler_params=params,
        name="pack",
    )(send_ids[0].T, cell_send_ids[0].T, parent_of, parent_centers, positions, masses.reshape(1, own))

    def exchange(blocks):
        flat = blocks.reshape(chips, -1, 128)
        came = lax.all_to_all(flat, "dom", split_axis=0, concat_axis=0, tiled=True)
        return came.reshape(blocks.shape)

    pool = exchange(first)

    part = pl.pallas_call(
        local_kernel,
        in_specs=[SMEM, SMEM, SMEM, VMEM, VMEM, VMEM],
        out_specs=VMEM,
        out_shape=shape(2, 3, own),
        scratch_shapes=[target_scratch, name_scratch],
        compiler_params=params,
        cost_estimate=pl.CostEstimate(flops=2 << 30, transcendentals=1 << 27, bytes_accessed=1 << 20),
        name="near_local",
    )(me, active, local_list.T, positions, other, tiles)

    pool, second, part = lax.optimization_barrier((pool, second, part))
    late_pool = exchange(second)

    part, owned = pl.pallas_call(
        far_kernel,
        in_specs=[SMEM, SMEM, SMEM, VMEM, VMEM, VMEM, VMEM],
        out_specs=[VMEM, VMEM],
        out_shape=[shape(2, 3, own), shape(8, 128)],
        scratch_shapes=[target_scratch, pltpu.VMEM((24, 128), F32)],
        compiler_params=params,
        cost_estimate=pl.CostEstimate(flops=1 << 29, transcendentals=1 << 24, bytes_accessed=1 << 20),
        name="far",
    )(me, active, far_list.T, positions, other, pool, part)
    owned_came = lax.ppermute(owned, "sub", swap)

    def near_remote(source, part, base, stride, name):
        return pl.pallas_call(
            functools.partial(remote_kernel, base, 2, stride),
            in_specs=[SMEM, SMEM, SMEM, VMEM, VMEM, VMEM, VMEM],
            out_specs=VMEM,
            out_shape=shape(2, 3, own),
            scratch_shapes=[target_scratch, name_scratch],
            compiler_params=params,
            cost_estimate=pl.CostEstimate(
                flops=1 << 30, transcendentals=1 << 26, bytes_accessed=1 << 20
            ),
            name=name,
        )(me, active, near_list.T, positions, other, source.reshape(-1, 8, 128), part)

    part = near_remote(pool, part, 0, 3, "near_first")
    part = near_remote(late_pool, part, 2, 2, "near_second")

    came = lax.ppermute(part[1], "sub", swap)
    accel, parents = pl.pallas_call(
        finish_kernel,
        in_specs=[SMEM, SMEM, VMEM, VMEM, VMEM, VMEM, VMEM],
        out_specs=[VMEM, VMEM],
        out_shape=[shape(3, own), shape(35, 16)],
        compiler_params=params,
        name="finish",
    )(me, active, part, came, old_accel, owned, owned_came)
    return accel, parents


def solution(mesh):
    both = ("dom", "sub")
    in_specs = (
        P(None, both),
        P(both),
        P(None, both),
        P("dom"),
        P(both),
        P(),
        P("dom", None),
        P("dom", None),
        P("dom", None),
        P(both, None, None),
        P(both, None, None),
    )
    out_specs = (P(None, both), P(None, "dom"))
    return jax.shard_map(local, mesh=mesh, in_specs=in_specs, out_specs=out_specs, check_vma=False)
```

```python
import functools

import jax
import jax.numpy as jnp
from jax import lax
from jax.experimental import pallas as pl
from jax.experimental.pallas import tpu as pltpu
from jax.sharding import PartitionSpec as P

BUCKET = 256
NB = 32
RQ = 4
RQC = 8
CELL_LANE = 70
EARLY = 1
USES = 2 * NB * 8
SOFT_SQ = 0.0025
FAR_SQ = 0.25
F32 = jnp.float32
SMEM = pl.BlockSpec(memory_space=pltpu.SMEM)
VMEM = pl.BlockSpec(memory_space=pltpu.VMEM)


def exponent_rows():
    listing = []
    for degree in range(5):
        for power_x in range(degree, -1, -1):
            for power_y in range(degree - power_x, -1, -1):
                listing.append((power_x, power_y, degree - power_x - power_y))
    return listing


TRIPLES = exponent_rows()
SPOT = {triple: number for number, triple in enumerate(TRIPLES)}
AXES = ((1, 0, 0), (0, 1, 0), (0, 0, 1))


def plus(*triples):
    return tuple(sum(parts) for parts in zip(*triples))


def lanes_of(ref, comp, b):
    return ref[comp : comp + 1, pl.ds(pl.multiple_of(b * BUCKET, BUCKET), BUCKET)]


def monomial_sums(offsets, mass):
    x, y, z = offsets
    known = {(0, 0, 0): mass}
    sums = []
    for triple in TRIPLES:
        if triple not in known:
            axis = next(a for a in range(3) if triple[a] > 0)
            lower = tuple(p - (1 if a == axis else 0) for a, p in enumerate(triple))
            known[triple] = known[lower] * offsets[axis]
        sums.append(jnp.sum(known[triple], axis=1, keepdims=True))
    return sums


def cell_columns(moments, center):
    m = {triple: moments[number] for number, triple in enumerate(TRIPLES)}
    trace1 = [sum(m[plus(e, f, f)] for f in AXES) for e in AXES]
    pairs = [t for t in TRIPLES if sum(t) == 2]
    trace2 = [sum(m[plus(t, f, f)] for f in AXES) for t in pairs]
    full = trace2[0] + trace2[3] + trace2[5]
    scale = (1.0, 1.0, 1.5, 2.5, 4.375)
    columns = [m[t] * scale[sum(t)] for t in TRIPLES]
    columns += center
    columns += [-0.5 * (m[(2, 0, 0)] + m[(0, 2, 0)] + m[(0, 0, 2)])]
    columns += [1.5 * t for t in trace1]
    columns += [3.75 * t for t in trace2]
    columns += [0.375 * full]
    return columns


def spread(columns, lane):
    table = jnp.zeros(lane.shape, F32)
    for number, column in enumerate(columns):
        table = jnp.where(lane == number, column, table)
    return table


def pack_kernel(
    ids_ref,
    cell_ids_ref,
    parent_ref,
    pcent_ref,
    pos_ref,
    mass_ref,
    tiles_ref,
    first_ref,
    second_ref,
    rows,
    about,
    terms,
    cells,
    contrib,
):
    chips = first_ref.shape[0]
    for b in range(NB):
        at = pl.ds(b * BUCKET, BUCKET)
        for comp in range(4):
            row = pos_ref[comp : comp + 1, at] if comp < 3 else mass_ref[0:1, at]
            rows[comp, b : b + 1, :] = row
            tiles_ref[b, 2 * comp : 2 * comp + 1, :] = row[:, :128]
            tiles_ref[b, 2 * comp + 1 : 2 * comp + 2, :] = row[:, 128:]
        parent = parent_ref[b]
        for comp in range(3):
            about[comp, b : b + 1, :] = jnp.full((1, 128), pcent_ref[comp, parent], F32)
    lane = lax.broadcasted_iota(jnp.int32, (NB, 128), 1)

    coords = [rows[comp] for comp in range(3)]
    centers = [jnp.sum(c, axis=1, keepdims=True) * (1.0 / BUCKET) for c in coords]
    sums = monomial_sums([c - o for c, o in zip(coords, centers)], rows[3])
    cells[...] = spread(cell_columns(sums, centers), lane - CELL_LANE)
    parents = [about[comp, :, 0:1] for comp in range(3)]
    sums = monomial_sums([c - o for c, o in zip(coords, parents)], rows[3])
    terms[0] = spread(sums, lane)
    terms[1] = pltpu.roll(terms[0], 35, 1)
    contrib[...] = jnp.zeros(contrib.shape, F32)
    for b in range(NB):
        parent = parent_ref[b]
        row = pl.ds((parent // 16) * 8 + parent % 8, 1)
        contrib[row, :] = contrib[row, :] + terms[(parent % 16) // 8, b : b + 1, :]

    def fill(step, carry):
        for part in range(2):
            dest = step * 2 + part
            for slot in range(RQ):
                tile = tiles_ref[jnp.maximum(ids_ref[slot, dest], 0)]
                if slot < EARLY:
                    first_ref[dest, slot] = tile
                else:
                    second_ref[dest, slot - EARLY] = tile
            for slot in range(RQC):
                cell = cells[pl.ds(jnp.maximum(cell_ids_ref[slot, dest], 0), 1), :]
                first_ref[dest, EARLY, slot : slot + 1, :] = cell
            own = contrib[pl.ds(pl.multiple_of(dest * 8, 8), 8), :]
            first_ref[dest, EARLY] = first_ref[dest, EARLY] + own
        return carry

    lax.fori_loop(0, chips // 2, fill, 0)


def spread_group(tile_ref, number, spread_ref):
    for r in range(8):
        row = tile_ref[number, r : r + 1, :]
        spread_ref[r] = jnp.transpose(jnp.broadcast_to(row, (128, 128)))


def add_pair(spread_ref, targets, sums, row):
    tx, ty, tz = load_targets(targets, jnp.minimum(row // NB, 1), row % NB)
    ax, ay, az = [sums[row, comp] for comp in range(3)]
    for h in range(2):
        for g in range(16):
            at = slice(8 * g, 8 * g + 8)
            sx, sy, sz, sm = [spread_ref[2 * comp + h, at, :] for comp in range(4)]
            sx, sy, sz, sm = [jnp.concatenate([v, v], axis=1) for v in (sx, sy, sz, sm)]
            dx = sx - tx
            dy = sy - ty
            dz = sz - tz
            inv = lax.rsqrt(dx * dx + dy * dy + (dz * dz + SOFT_SQ))
            weight = sm * inv * (inv * inv)
            ax = ax + weight * dx
            ay = ay + weight * dy
            az = az + weight * dz
    for comp, value in enumerate((ax, ay, az)):
        sums[row, comp] = value


def start_sums(sub, act_ref, sums, note, carry):
    def step(row, carry):
        half = row // NB
        listed = jnp.where(half == 0, sub, 1 - sub) * NB + row % NB

        def live(carry):
            for comp in range(3):
                sums[row, comp] = jnp.zeros((8, BUCKET), F32)
            return note(row, listed, carry)

        return lax.cond(act_ref[listed] > 0, live, lambda carry: carry, carry)

    return lax.fori_loop(0, 2 * NB, step, carry)


def end_sums(sub, act_ref, sums, out_ref):
    def visit(half, b, row):
        add_rows(out_ref, half, b, [sums[half * NB + b, comp] for comp in range(3)])

    each_active(sub, act_ref, visit)


def each_active(sub, act_ref, visit):
    def step(t, carry):
        half = t // NB
        b = t % NB
        row = jnp.where(half == 0, sub, 1 - sub) * NB + b

        @pl.when(act_ref[row] > 0)
        def _():
            visit(half, b, row)

        return carry

    lax.fori_loop(0, 2 * NB, step, 0)


def load_targets(targets, half, b):
    return [
        jnp.broadcast_to(lanes_of(targets.at[half], comp, b), (8, BUCKET)) for comp in range(3)
    ]


def add_rows(ref, half, b, values):
    at = pl.ds(pl.multiple_of(b * BUCKET, BUCKET), BUCKET)
    for comp in range(3):
        row = jnp.sum(values[comp], axis=0, keepdims=True)
        ref[half, comp : comp + 1, at] = ref[half, comp : comp + 1, at] + row


def local_kernel(
    sub_ref, act_ref, list_ref, pos_ref, other_ref, tiles_ref, out_ref, targets, sums, one, two,
    users, counts,
):
    sub = sub_ref[0]
    targets[0] = pos_ref[...]
    targets[1] = other_ref[...]
    out_ref[...] = jnp.zeros(out_ref.shape, F32)
    for comp in range(3):
        sums[2 * NB, comp] = jnp.zeros((8, BUCKET), F32)
    for b in range(NB + 1):
        counts[b] = 0
        users[b * USES] = 2 * NB

    def note(row, listed, carry):
        for k in range(8):
            entry = list_ref[k, listed]
            group = jnp.where(entry // NB == sub, entry % NB, NB)
            users[group * USES + counts[group]] = row
            counts[group] = counts[group] + 1
        return carry

    start_sums(sub, act_ref, sums, note, 0)

    def work(group, now, later):
        spread_group(tiles_ref, jnp.minimum(group + 1, NB - 1), later)
        add_pair(now, targets, sums, users[group * USES])

        def more(use, carry):
            add_pair(now, targets, sums, users[group * USES + use])
            return carry

        lax.fori_loop(1, counts[group], more, 0)

    spread_group(tiles_ref, 0, one)

    def step(pair, carry):
        work(2 * pair, one, two)
        work(2 * pair + 1, two, one)
        return carry

    lax.fori_loop(0, NB // 2, step, 0)
    end_sums(sub, act_ref, sums, out_ref)


def remote_kernel(base, width, stride, *refs):
    sub_ref, act_ref, list_ref, pos_ref, other_ref, pool_ref, part_ref, out_ref = refs[:8]
    targets, sums, one, two, names, homes = refs[8:]
    sub = sub_ref[0]
    targets[0] = pos_ref[...]
    targets[1] = other_ref[...]
    out_ref[...] = part_ref[...]

    def note(row, listed, count):
        for k in range(8):
            entry = list_ref[k, listed]
            slot = entry % RQ - base
            names[count] = (entry // (2 * RQ)) * stride + slot
            homes[count] = row
            mine = ((entry // RQ) % 2 == sub) & (slot >= 0) & (slot < width)
            count = count + jnp.where(mine, 1, 0)
        return count

    count = start_sums(sub, act_ref, sums, note, jnp.int32(0))

    @pl.when(count > 0)
    def _():
        spread_group(pool_ref, names[0], one)

        def step(pair, carry):
            spread_group(pool_ref, names[2 * pair + 1], two)
            add_pair(one, targets, sums, homes[2 * pair])
            spread_group(pool_ref, names[jnp.minimum(2 * pair + 2, count - 1)], one)
            add_pair(two, targets, sums, homes[2 * pair + 1])
            return carry

        lax.fori_loop(0, count // 2, step, 0)

        @pl.when(count % 2 == 1)
        def _():
            add_pair(one, targets, sums, homes[count - 1])

    end_sums(sub, act_ref, sums, out_ref)


def contract(tensor, axis, weighted):
    total = None
    for triple, value in weighted.items():
        term = tensor[plus(triple, AXES[axis])] * value
        total = term if total is None else total + term
    return total


def cell_pull(table, targets):
    def column(number):
        return table[:, CELL_LANE + number : CELL_LANE + number + 1]

    m = {triple: column(number) for number, triple in enumerate(TRIPLES)}
    r = [targets[a] - column(35 + a) for a in range(3)]
    x, y, z = r
    rho_sq = x * x + y * y + (z * z + FAR_SQ)
    inv = lax.rsqrt(rho_sq)
    inv_sq = inv * inv
    u = [inv]
    for _ in range(5):
        u.append(u[-1] * inv_sq)
    xx, yy, zz, xy, xz, yz = x * x, y * y, z * z, x * y, x * z, y * z
    first = {(1, 0, 0): x, (0, 1, 0): y, (0, 0, 1): z}
    second = {
        (2, 0, 0): xx,
        (1, 1, 0): 2.0 * xy,
        (1, 0, 1): 2.0 * xz,
        (0, 2, 0): yy,
        (0, 1, 1): 2.0 * yz,
        (0, 0, 2): zz,
    }
    x3, y3, z3 = 3.0 * x, 3.0 * y, 3.0 * z
    third = {
        (3, 0, 0): xx * x,
        (2, 1, 0): xx * y3,
        (2, 0, 1): xx * z3,
        (1, 2, 0): yy * x3,
        (1, 1, 1): xy * (2.0 * z3),
        (1, 0, 2): zz * x3,
        (0, 3, 0): yy * y,
        (0, 2, 1): yy * z3,
        (0, 1, 2): zz * y3,
        (0, 0, 3): zz * z,
    }
    pairs = [t for t in TRIPLES if sum(t) == 2]
    trace2 = {t: column(42 + number) for number, t in enumerate(pairs)}
    grad = []
    q1, q2, q3, q4 = column(38), column(48), None, None
    for a in range(3):
        m1 = m[AXES[a]]
        a2 = contract(m, a, first)
        b2 = column(39 + a)
        a3 = contract(m, a, second)
        b3 = contract(trace2, a, first)
        a4 = contract(m, a, third)
        grad.append(
            m1 * u[1]
            + (a2 + (a2 - b2)) * u[2]
            + (a3 + 2.0 * (a3 - b3)) * u[3]
            + (4.0 * a4) * u[4]
        )
        q1 = q1 + r[a] * m1
        q2 = q2 + r[a] * (a2 - b2)
        low, high = r[a] * (a3 - b3), r[a] * a4
        q3 = low if q3 is None else q3 + low
        q4 = high if q4 is None else q4 + high
    pull = (
        m[(0, 0, 0)] * u[1] + 3.0 * q1 * u[2] + 5.0 * q2 * u[3] + 7.0 * q3 * u[4] + 9.0 * q4 * u[5]
    )
    return [grad[a] - r[a] * pull for a in range(3)]


def far_kernel(
    sub_ref,
    act_ref,
    list_ref,
    pos_ref,
    other_ref,
    pool_ref,
    part_ref,
    out_ref,
    owned_ref,
    targets,
    picked,
):
    sub = sub_ref[0]
    targets[0] = pos_ref[...]
    targets[1] = other_ref[...]
    out_ref[...] = part_ref[...]

    def gather_owned(step, total):
        for part in range(2):
            total = total + pool_ref[step * 2 + part, EARLY]
        return total

    chips = pool_ref.shape[0]
    owned_ref[...] = lax.fori_loop(0, chips // 2, gather_owned, jnp.zeros((8, 128), F32))

    def visit(half, b, row):
        picked[...] = jnp.zeros(picked.shape, F32)
        count = 0
        for k in range(16):
            entry = list_ref[k, row]
            cell = pool_ref[entry // (2 * RQC), EARLY, pl.ds(entry % RQC, 1), :]
            mine = (entry // RQC) % 2 == sub
            picked[pl.ds(count, 1), :] = jnp.where(mine, cell, 0.0)
            count = count + jnp.where(mine, 1, 0)
        sides = load_targets(targets, half, b)

        def add_cells(step, sums):
            table = picked[pl.ds(pl.multiple_of(step * 8, 8), 8), :]
            return tuple(s + p for s, p in zip(sums, cell_pull(table, sides)))

        zero = jnp.zeros((8, BUCKET), F32)
        sums = lax.fori_loop(0, (count + 7) // 8, add_cells, (zero, zero, zero))
        add_rows(out_ref, half, b, sums)

    each_active(sub, act_ref, visit)


def finish_kernel(
    sub_ref, act_ref, part_ref, came_ref, old_ref, mom_ref, mom_came_ref, accel_ref, parent_ref
):
    sub = sub_ref[0]
    for b in range(NB):
        at = pl.ds(b * BUCKET, BUCKET)
        live = act_ref[sub * NB + b] > 0
        accel_ref[:, at] = jnp.where(live, part_ref[0, :, at] + came_ref[:, at], old_ref[:, at])
    both = (mom_ref[...] + mom_came_ref[...]).T
    parent_ref[:, 0:8] = both[0:35]
    parent_ref[:, 8:16] = both[35:70]


def shape(*dims):
    return jax.ShapeDtypeStruct(dims, F32)


def local(
    positions,
    masses,
    old_accel,
    active,
    parent_of,
    parent_centers,
    local_list,
    near_list,
    far_list,
    send_ids,
    cell_send_ids,
):
    chips = lax.axis_size("dom")
    own = NB * BUCKET
    me = lax.axis_index("sub").astype(jnp.int32).reshape(1)
    swap = [(0, 1), (1, 0)]
    target_scratch = pltpu.VMEM((2, 3, own), F32)
    near_scratch = [
        target_scratch,
        pltpu.VMEM((2 * NB + 1, 3, 8, BUCKET), F32),
        pltpu.VMEM((8, 128, 128), F32),
        pltpu.VMEM((8, 128, 128), F32),
    ]
    params = pltpu.CompilerParams(vmem_limit_bytes=32 << 20)

    other = lax.ppermute(positions, "sub", swap)

    tiles, first, second = pl.pallas_call(
        pack_kernel,
        in_specs=[SMEM, SMEM, SMEM, SMEM, VMEM, VMEM],
        out_specs=[VMEM, VMEM, VMEM],
        out_shape=[shape(NB, 8, 128), shape(chips, EARLY + 1, 8, 128), shape(chips, RQ - EARLY, 8, 128)],
        scratch_shapes=[
            pltpu.VMEM((4, NB, BUCKET), F32),
            pltpu.VMEM((3, NB, 128), F32),
            pltpu.VMEM((2, NB, 128), F32),
            pltpu.VMEM((NB, 128), F32),
            pltpu.VMEM((chips * 8, 128), F32),
        ],
        compiler_params=params,
        name="pack",
    )(send_ids[0].T, cell_send_ids[0].T, parent_of, parent_centers, positions, masses.reshape(1, own))

    def exchange(blocks):
        flat = blocks.reshape(chips, -1, 128)
        came = lax.all_to_all(flat, "dom", split_axis=0, concat_axis=0, tiled=True)
        return came.reshape(blocks.shape)

    pool = exchange(first)

    part = pl.pallas_call(
        local_kernel,
        in_specs=[SMEM, SMEM, SMEM, VMEM, VMEM, VMEM],
        out_specs=VMEM,
        out_shape=shape(2, 3, own),
        scratch_shapes=near_scratch
        + [pltpu.SMEM(((NB + 1) * USES,), jnp.int32), pltpu.SMEM((NB + 1,), jnp.int32)],
        compiler_params=params,
        cost_estimate=pl.CostEstimate(flops=2 << 30, transcendentals=1 << 27, bytes_accessed=1 << 20),
        name="near_local",
    )(me, active, local_list.T, positions, other, tiles)

    pool, second, part = lax.optimization_barrier((pool, second, part))
    late_pool = exchange(second)

    part, owned = pl.pallas_call(
        far_kernel,
        in_specs=[SMEM, SMEM, SMEM, VMEM, VMEM, VMEM, VMEM],
        out_specs=[VMEM, VMEM],
        out_shape=[shape(2, 3, own), shape(8, 128)],
        scratch_shapes=[target_scratch, pltpu.VMEM((24, 128), F32)],
        compiler_params=params,
        cost_estimate=pl.CostEstimate(flops=1 << 29, transcendentals=1 << 24, bytes_accessed=1 << 20),
        name="far",
    )(me, active, far_list.T, positions, other, pool, part)
    owned_came = lax.ppermute(owned, "sub", swap)

    def near_remote(source, part, base, width, stride, name):
        return pl.pallas_call(
            functools.partial(remote_kernel, base, width, stride),
            in_specs=[SMEM, SMEM, SMEM, VMEM, VMEM, VMEM, VMEM],
            out_specs=VMEM,
            out_shape=shape(2, 3, own),
            scratch_shapes=near_scratch + [pltpu.SMEM((USES + 8,), jnp.int32)] * 2,
            compiler_params=params,
            cost_estimate=pl.CostEstimate(
                flops=1 << 30, transcendentals=1 << 26, bytes_accessed=1 << 20
            ),
            name=name,
        )(me, active, near_list.T, positions, other, source.reshape(-1, 8, 128), part)

    part = near_remote(pool, part, 0, EARLY, EARLY + 1, "near_first")
    part = near_remote(late_pool, part, EARLY, RQ - EARLY, RQ - EARLY, "near_second")

    came = lax.ppermute(part[1], "sub", swap)
    accel, parents = pl.pallas_call(
        finish_kernel,
        in_specs=[SMEM, SMEM, VMEM, VMEM, VMEM, VMEM, VMEM],
        out_specs=[VMEM, VMEM],
        out_shape=[shape(3, own), shape(35, 16)],
        compiler_params=params,
        name="finish",
    )(me, active, part, came, old_accel, owned, owned_came)
    return accel, parents


def solution(mesh):
    both = ("dom", "sub")
    in_specs = (
        P(None, both),
        P(both),
        P(None, both),
        P("dom"),
        P(both),
        P(),
        P("dom", None),
        P("dom", None),
        P("dom", None),
        P(both, None, None),
        P(both, None, None),
    )
    out_specs = (P(None, both), P(None, "dom"))
    return jax.shard_map(local, mesh=mesh, in_specs=in_specs, out_specs=out_specs, check_vma=False)
```

```python
import functools

import jax
import jax.numpy as jnp
from jax import lax
from jax.experimental import pallas as pl
from jax.experimental.pallas import tpu as pltpu
from jax.sharding import PartitionSpec as P

BUCKET = 256
NB = 32
RQ = 4
RQC = 8
CELL_LANE = 70
EARLY = 1
USES_BITS = 9
USES = 1 << USES_BITS
SOFT_SQ = 0.0025
FAR_SQ = 0.25
F32 = jnp.float32
SMEM = pl.BlockSpec(memory_space=pltpu.SMEM)
VMEM = pl.BlockSpec(memory_space=pltpu.VMEM)


def exponent_rows():
    listing = []
    for degree in range(5):
        for power_x in range(degree, -1, -1):
            for power_y in range(degree - power_x, -1, -1):
                listing.append((power_x, power_y, degree - power_x - power_y))
    return listing


TRIPLES = exponent_rows()
SPOT = {triple: number for number, triple in enumerate(TRIPLES)}
AXES = ((1, 0, 0), (0, 1, 0), (0, 0, 1))


def plus(*triples):
    return tuple(sum(parts) for parts in zip(*triples))


def lanes_of(ref, comp, b):
    return ref[comp : comp + 1, pl.ds(pl.multiple_of(b * BUCKET, BUCKET), BUCKET)]


def monomial_sums(offsets, mass):
    x, y, z = offsets
    known = {(0, 0, 0): mass}
    sums = []
    for triple in TRIPLES:
        if triple not in known:
            axis = next(a for a in range(3) if triple[a] > 0)
            lower = tuple(p - (1 if a == axis else 0) for a, p in enumerate(triple))
            known[triple] = known[lower] * offsets[axis]
        sums.append(jnp.sum(known[triple], axis=1, keepdims=True))
    return sums


def cell_columns(moments, center):
    m = {triple: moments[number] for number, triple in enumerate(TRIPLES)}
    trace1 = [sum(m[plus(e, f, f)] for f in AXES) for e in AXES]
    pairs = [t for t in TRIPLES if sum(t) == 2]
    trace2 = [sum(m[plus(t, f, f)] for f in AXES) for t in pairs]
    full = trace2[0] + trace2[3] + trace2[5]
    scale = (1.0, 1.0, 1.5, 2.5, 4.375)
    columns = [m[t] * scale[sum(t)] for t in TRIPLES]
    columns += center
    columns += [-0.5 * (m[(2, 0, 0)] + m[(0, 2, 0)] + m[(0, 0, 2)])]
    columns += [1.5 * t for t in trace1]
    columns += [3.75 * t for t in trace2]
    columns += [0.375 * full]
    return columns


def spread(columns, lane):
    table = jnp.zeros(lane.shape, F32)
    for number, column in enumerate(columns):
        table = jnp.where(lane == number, column, table)
    return table


def pack_kernel(
    ids_ref,
    cell_ids_ref,
    parent_ref,
    pcent_ref,
    pos_ref,
    mass_ref,
    tiles_ref,
    first_ref,
    second_ref,
    rows,
    about,
    terms,
    cells,
    contrib,
):
    chips = first_ref.shape[0]
    for b in range(NB):
        at = pl.ds(b * BUCKET, BUCKET)
        for comp in range(4):
            row = pos_ref[comp : comp + 1, at] if comp < 3 else mass_ref[0:1, at]
            rows[comp, b : b + 1, :] = row
            tiles_ref[b, 2 * comp : 2 * comp + 1, :] = row[:, :128]
            tiles_ref[b, 2 * comp + 1 : 2 * comp + 2, :] = row[:, 128:]
        parent = parent_ref[b]
        for comp in range(3):
            about[comp, b : b + 1, :] = jnp.full((1, 128), pcent_ref[comp, parent], F32)
    lane = lax.broadcasted_iota(jnp.int32, (NB, 128), 1)

    coords = [rows[comp] for comp in range(3)]
    centers = [jnp.sum(c, axis=1, keepdims=True) * (1.0 / BUCKET) for c in coords]
    sums = monomial_sums([c - o for c, o in zip(coords, centers)], rows[3])
    cells[...] = spread(cell_columns(sums, centers), lane - CELL_LANE)
    parents = [about[comp, :, 0:1] for comp in range(3)]
    sums = monomial_sums([c - o for c, o in zip(coords, parents)], rows[3])
    terms[0] = spread(sums, lane)
    terms[1] = pltpu.roll(terms[0], 35, 1)
    contrib[...] = jnp.zeros(contrib.shape, F32)
    for b in range(NB):
        parent = parent_ref[b]
        row = pl.ds(((parent >> 4) << 3) + (parent & 7), 1)
        contrib[row, :] = contrib[row, :] + terms[(parent >> 3) & 1, b : b + 1, :]

    def fill(step, carry):
        for part in range(2):
            dest = step * 2 + part
            for slot in range(RQ):
                tile = tiles_ref[jnp.maximum(ids_ref[slot, dest], 0)]
                if slot < EARLY:
                    first_ref[dest, slot] = tile
                else:
                    second_ref[dest, slot - EARLY] = tile
            for slot in range(RQC):
                cell = cells[pl.ds(jnp.maximum(cell_ids_ref[slot, dest], 0), 1), :]
                first_ref[dest, EARLY, slot : slot + 1, :] = cell
            own = contrib[pl.ds(pl.multiple_of(dest * 8, 8), 8), :]
            first_ref[dest, EARLY] = first_ref[dest, EARLY] + own
        return carry

    lax.fori_loop(0, chips // 2, fill, 0)


def spread_group(tile_ref, number, spread_ref):
    for r in range(8):
        row = tile_ref[number, r : r + 1, :]
        spread_ref[r] = jnp.transpose(jnp.broadcast_to(row, (128, 128)))


def add_pair(spread_ref, targets, sums, row):
    tx, ty, tz = load_targets(targets, jnp.minimum(row >> 5, 1), row & 31)
    ax, ay, az = [sums[row, comp] for comp in range(3)]
    for h in range(2):
        for g in range(16):
            at = slice(8 * g, 8 * g + 8)
            sx, sy, sz, sm = [spread_ref[2 * comp + h, at, :] for comp in range(4)]
            sx, sy, sz, sm = [jnp.concatenate([v, v], axis=1) for v in (sx, sy, sz, sm)]
            dx = sx - tx
            dy = sy - ty
            dz = sz - tz
            inv = lax.rsqrt(dx * dx + dy * dy + (dz * dz + SOFT_SQ))
            weight = sm * inv * (inv * inv)
            ax = ax + weight * dx
            ay = ay + weight * dy
            az = az + weight * dz
    for comp, value in enumerate((ax, ay, az)):
        sums[row, comp] = value


def list_active(sub, act_ref, order):
    total = 0
    for row in range(2 * NB):
        listed = (sub if row < NB else 1 - sub) * NB + row % NB
        order[total] = row
        total = total + act_ref[listed]
    return total


def listed_row(sub, row):
    return row ^ (sub << 5)


def start_sums(order, total, sums, note, carry):
    def step(n, carry):
        row = order[n]
        for comp in range(3):
            sums[row, comp] = jnp.zeros((8, BUCKET), F32)
        return note(row, carry)

    return lax.fori_loop(0, total, step, carry)


def end_sums(order, total, sums, out_ref):
    def step(n, carry):
        row = order[n]
        add_rows(out_ref, row >> 5, row & 31, [sums[row, comp] for comp in range(3)])
        return carry

    lax.fori_loop(0, total, step, 0)


def load_targets(targets, half, b):
    return [
        jnp.broadcast_to(lanes_of(targets.at[half], comp, b), (8, BUCKET)) for comp in range(3)
    ]


def add_rows(ref, half, b, values):
    at = pl.ds(pl.multiple_of(b * BUCKET, BUCKET), BUCKET)
    for comp in range(3):
        row = jnp.sum(values[comp], axis=0, keepdims=True)
        ref[half, comp : comp + 1, at] = ref[half, comp : comp + 1, at] + row


def local_kernel(
    sub_ref, act_ref, list_ref, pos_ref, other_ref, tiles_ref, out_ref, targets, order, sums,
    one, two, users, counts,
):
    sub = sub_ref[0]
    targets[0] = pos_ref[...]
    targets[1] = other_ref[...]
    out_ref[...] = jnp.zeros(out_ref.shape, F32)
    for comp in range(3):
        sums[2 * NB, comp] = jnp.zeros((8, BUCKET), F32)
    for b in range(NB + 1):
        counts[b] = 0
        users[b * USES] = 2 * NB
    total = list_active(sub, act_ref, order)

    def note(row, carry):
        listed = listed_row(sub, row)
        for k in range(8):
            entry = list_ref[k, listed]
            group = jnp.where((entry >> 5) == sub, entry & 31, NB)
            count = counts[group]
            users[(group << USES_BITS) + count] = row
            counts[group] = count + 1
        return carry

    start_sums(order, total, sums, note, 0)

    def work(group, now, later):
        spread_group(tiles_ref, jnp.minimum(group + 1, NB - 1), later)
        first = group << USES_BITS
        add_pair(now, targets, sums, users[first])

        def more(use, carry):
            add_pair(now, targets, sums, users[first + use])
            return carry

        lax.fori_loop(1, counts[group], more, 0)

    spread_group(tiles_ref, 0, one)

    def step(pair, carry):
        work(2 * pair, one, two)
        work(2 * pair + 1, two, one)
        return carry

    lax.fori_loop(0, NB // 2, step, 0)
    end_sums(order, total, sums, out_ref)


def near_pairs(base, width, stride, sub, total, list_ref, pool_ref, out_ref, scratch):
    targets, order, sums, one, two, names, homes = scratch

    def note(row, count):
        listed = listed_row(sub, row)
        for k in range(8):
            entry = list_ref[k, listed]
            slot = (entry & (RQ - 1)) - base
            names[count] = (entry >> 3) * stride + slot
            homes[count] = row
            mine = (((entry >> 2) & 1) == sub) & (slot >= 0) & (slot < width)
            count = count + jnp.where(mine, 1, 0)
        return count

    count = start_sums(order, total, sums, note, jnp.int32(0))

    @pl.when(count > 0)
    def _():
        spread_group(pool_ref, names[0], one)

        def step(pair, carry):
            spread_group(pool_ref, names[2 * pair + 1], two)
            add_pair(one, targets, sums, homes[2 * pair])
            spread_group(pool_ref, names[jnp.minimum(2 * pair + 2, count - 1)], one)
            add_pair(two, targets, sums, homes[2 * pair + 1])
            return carry

        lax.fori_loop(0, count >> 1, step, 0)

        @pl.when((count & 1) == 1)
        def _():
            add_pair(one, targets, sums, homes[count - 1])

    end_sums(order, total, sums, out_ref)


def late_kernel(
    sub_ref, act_ref, list_ref, pos_ref, other_ref, pool_ref, part_ref, out_ref, targets, order,
    sums, one, two, names, homes,
):
    sub = sub_ref[0]
    targets[0] = pos_ref[...]
    targets[1] = other_ref[...]
    out_ref[...] = part_ref[...]
    total = list_active(sub, act_ref, order)
    scratch = (targets, order, sums, one, two, names, homes)
    wide = RQ - EARLY
    near_pairs(EARLY, wide, wide, sub, total, list_ref, pool_ref, out_ref, scratch)


def contract(tensor, axis, weighted):
    total = None
    for triple, value in weighted.items():
        term = tensor[plus(triple, AXES[axis])] * value
        total = term if total is None else total + term
    return total


def cell_pull(table, targets):
    def column(number):
        return table[:, CELL_LANE + number : CELL_LANE + number + 1]

    m = {triple: column(number) for number, triple in enumerate(TRIPLES)}
    r = [targets[a] - column(35 + a) for a in range(3)]
    x, y, z = r
    rho_sq = x * x + y * y + (z * z + FAR_SQ)
    inv = lax.rsqrt(rho_sq)
    inv_sq = inv * inv
    u = [inv]
    for _ in range(5):
        u.append(u[-1] * inv_sq)
    xx, yy, zz, xy, xz, yz = x * x, y * y, z * z, x * y, x * z, y * z
    first = {(1, 0, 0): x, (0, 1, 0): y, (0, 0, 1): z}
    second = {
        (2, 0, 0): xx,
        (1, 1, 0): 2.0 * xy,
        (1, 0, 1): 2.0 * xz,
        (0, 2, 0): yy,
        (0, 1, 1): 2.0 * yz,
        (0, 0, 2): zz,
    }
    x3, y3, z3 = 3.0 * x, 3.0 * y, 3.0 * z
    third = {
        (3, 0, 0): xx * x,
        (2, 1, 0): xx * y3,
        (2, 0, 1): xx * z3,
        (1, 2, 0): yy * x3,
        (1, 1, 1): xy * (2.0 * z3),
        (1, 0, 2): zz * x3,
        (0, 3, 0): yy * y,
        (0, 2, 1): yy * z3,
        (0, 1, 2): zz * y3,
        (0, 0, 3): zz * z,
    }
    pairs = [t for t in TRIPLES if sum(t) == 2]
    trace2 = {t: column(42 + number) for number, t in enumerate(pairs)}
    grad = []
    q1, q2, q3, q4 = column(38), column(48), None, None
    for a in range(3):
        m1 = m[AXES[a]]
        a2 = contract(m, a, first)
        b2 = column(39 + a)
        a3 = contract(m, a, second)
        b3 = contract(trace2, a, first)
        a4 = contract(m, a, third)
        grad.append(
            m1 * u[1]
            + (a2 + (a2 - b2)) * u[2]
            + (a3 + 2.0 * (a3 - b3)) * u[3]
            + (4.0 * a4) * u[4]
        )
        q1 = q1 + r[a] * m1
        q2 = q2 + r[a] * (a2 - b2)
        low, high = r[a] * (a3 - b3), r[a] * a4
        q3 = low if q3 is None else q3 + low
        q4 = high if q4 is None else q4 + high
    pull = (
        m[(0, 0, 0)] * u[1] + 3.0 * q1 * u[2] + 5.0 * q2 * u[3] + 7.0 * q3 * u[4] + 9.0 * q4 * u[5]
    )
    return [grad[a] - r[a] * pull for a in range(3)]


def far_cells(sub, total, list_ref, pool_ref, out_ref, targets, order, picked):
    place = lax.broadcasted_iota(jnp.int32, (8, 128), 0)

    def visit(n, carry):
        row = order[n]
        listed = listed_row(sub, row)
        count = 0
        for k in range(16):
            entry = list_ref[k, listed]
            at = pl.ds(count, 1)
            picked[at, :] = pool_ref[((entry >> 4) << 1) + EARLY, pl.ds(entry & (RQC - 1), 1), :]
            count = count + jnp.where(((entry >> 3) & 1) == sub, 1, 0)
        half, b = row >> 5, row & 31
        sides = load_targets(targets, half, b)

        def add_cells(step, sums):
            table = picked[pl.ds(pl.multiple_of(step * 8, 8), 8), :]
            table = jnp.where(place < count - step * 8, table, 0.0)
            return tuple(s + p for s, p in zip(sums, cell_pull(table, sides)))

        zero = jnp.zeros((8, BUCKET), F32)
        sums = lax.fori_loop(0, (count + 7) >> 3, add_cells, (zero, zero, zero))
        add_rows(out_ref, half, b, sums)
        return carry

    lax.fori_loop(0, total, visit, 0)


def early_kernel(
    sub_ref, act_ref, near_ref, far_ref, pos_ref, other_ref, pool_ref, part_ref, out_ref,
    owned_ref, targets, order, sums, one, two, names, homes, picked,
):
    sub = sub_ref[0]
    targets[0] = pos_ref[...]
    targets[1] = other_ref[...]
    out_ref[...] = part_ref[...]

    def gather_owned(step, total):
        for part in range(4):
            total = total + pool_ref[(step * 4 + part) * (EARLY + 1) + EARLY]
        return total

    chips = pool_ref.shape[0] // (EARLY + 1)
    owned_ref[...] = lax.fori_loop(0, chips // 4, gather_owned, jnp.zeros((8, 128), F32))
    total = list_active(sub, act_ref, order)
    far_cells(sub, total, far_ref, pool_ref, out_ref, targets, order, picked)
    scratch = (targets, order, sums, one, two, names, homes)
    near_pairs(0, EARLY, EARLY + 1, sub, total, near_ref, pool_ref, out_ref, scratch)


def finish_kernel(
    sub_ref, act_ref, part_ref, came_ref, old_ref, mom_ref, mom_came_ref, accel_ref, parent_ref
):
    sub = sub_ref[0]
    for b in range(NB):
        at = pl.ds(b * BUCKET, BUCKET)
        live = act_ref[sub * NB + b] > 0
        accel_ref[:, at] = jnp.where(live, part_ref[0, :, at] + came_ref[:, at], old_ref[:, at])
    both = (mom_ref[...] + mom_came_ref[...]).T
    parent_ref[:, 0:8] = both[0:35]
    parent_ref[:, 8:16] = both[35:70]


def shape(*dims):
    return jax.ShapeDtypeStruct(dims, F32)


def local(
    positions,
    masses,
    old_accel,
    active,
    parent_of,
    parent_centers,
    local_list,
    near_list,
    far_list,
    send_ids,
    cell_send_ids,
):
    chips = lax.axis_size("dom")
    own = NB * BUCKET
    me = lax.axis_index("sub").astype(jnp.int32).reshape(1)
    swap = [(0, 1), (1, 0)]
    near_scratch = [
        pltpu.VMEM((2, 3, own), F32),
        pltpu.SMEM((2 * NB + 8,), jnp.int32),
        pltpu.VMEM((2 * NB + 1, 3, 8, BUCKET), F32),
        pltpu.VMEM((8, 128, 128), F32),
        pltpu.VMEM((8, 128, 128), F32),
    ]
    params = pltpu.CompilerParams(vmem_limit_bytes=32 << 20)

    other = lax.ppermute(positions, "sub", swap)

    tiles, first, second = pl.pallas_call(
        pack_kernel,
        in_specs=[SMEM, SMEM, SMEM, SMEM, VMEM, VMEM],
        out_specs=[VMEM, VMEM, VMEM],
        out_shape=[shape(NB, 8, 128), shape(chips, EARLY + 1, 8, 128), shape(chips, RQ - EARLY, 8, 128)],
        scratch_shapes=[
            pltpu.VMEM((4, NB, BUCKET), F32),
            pltpu.VMEM((3, NB, 128), F32),
            pltpu.VMEM((2, NB, 128), F32),
            pltpu.VMEM((NB, 128), F32),
            pltpu.VMEM((chips * 8, 128), F32),
        ],
        compiler_params=pltpu.CompilerParams(vmem_limit_bytes=60 << 20),
        name="pack",
    )(send_ids[0].T, cell_send_ids[0].T, parent_of, parent_centers, positions, masses.reshape(1, own))

    def exchange(blocks):
        flat = blocks.reshape(chips, -1, 128)
        came = lax.all_to_all(flat, "dom", split_axis=0, concat_axis=0, tiled=True)
        return came.reshape(blocks.shape)

    pool = exchange(first)

    part = pl.pallas_call(
        local_kernel,
        in_specs=[SMEM, SMEM, SMEM, VMEM, VMEM, VMEM],
        out_specs=VMEM,
        out_shape=shape(2, 3, own),
        scratch_shapes=near_scratch
        + [pltpu.SMEM(((NB + 1) * USES,), jnp.int32), pltpu.SMEM((NB + 1,), jnp.int32)],
        compiler_params=params,
        cost_estimate=pl.CostEstimate(flops=2 << 30, transcendentals=1 << 27, bytes_accessed=1 << 20),
        name="near_local",
    )(me, active, local_list.T, positions, other, tiles)

    pool, second, part = lax.optimization_barrier((pool, second, part))
    late_pool = exchange(second)

    pair_scratch = near_scratch + [pltpu.SMEM((USES + 8,), jnp.int32)] * 2
    part, owned = pl.pallas_call(
        early_kernel,
        in_specs=[SMEM, SMEM, SMEM, SMEM, VMEM, VMEM, VMEM, VMEM],
        out_specs=[VMEM, VMEM],
        out_shape=[shape(2, 3, own), shape(8, 128)],
        scratch_shapes=pair_scratch + [pltpu.VMEM((24, 128), F32)],
        compiler_params=params,
        cost_estimate=pl.CostEstimate(flops=2 << 30, transcendentals=1 << 27, bytes_accessed=1 << 20),
        name="early",
    )(me, active, near_list.T, far_list.T, positions, other, pool.reshape(-1, 8, 128), part)
    owned_came = lax.ppermute(owned, "sub", swap)

    part = pl.pallas_call(
        late_kernel,
        in_specs=[SMEM, SMEM, SMEM, VMEM, VMEM, VMEM, VMEM],
        out_specs=VMEM,
        out_shape=shape(2, 3, own),
        scratch_shapes=pair_scratch,
        compiler_params=params,
        cost_estimate=pl.CostEstimate(flops=1 << 30, transcendentals=1 << 26, bytes_accessed=1 << 20),
        name="late",
    )(me, active, near_list.T, positions, other, late_pool.reshape(-1, 8, 128), part)

    came = lax.ppermute(part[1], "sub", swap)
    accel, parents = pl.pallas_call(
        finish_kernel,
        in_specs=[SMEM, SMEM, VMEM, VMEM, VMEM, VMEM, VMEM],
        out_specs=[VMEM, VMEM],
        out_shape=[shape(3, own), shape(35, 16)],
        compiler_params=params,
        name="finish",
    )(me, active, part, came, old_accel, owned, owned_came)
    return accel, parents


def solution(mesh):
    both = ("dom", "sub")
    in_specs = (
        P(None, both),
        P(both),
        P(None, both),
        P("dom"),
        P(both),
        P(),
        P("dom", None),
        P("dom", None),
        P("dom", None),
        P(both, None, None),
        P(both, None, None),
    )
    out_specs = (P(None, both), P(None, "dom"))
    return jax.shard_map(local, mesh=mesh, in_specs=in_specs, out_specs=out_specs, check_vma=False)
```

```python
import functools

import jax
import jax.numpy as jnp
from jax import lax
from jax.experimental import pallas as pl
from jax.experimental.pallas import tpu as pltpu
from jax.sharding import PartitionSpec as P

BUCKET = 256
NB = 32
RQ = 4
RQC = 8
CELL_LANE = 70
EARLY = 2
USES_BITS = 9
USES = 1 << USES_BITS
SOFT_SQ = 0.0025
FAR_SQ = 0.25
F32 = jnp.float32
SMEM = pl.BlockSpec(memory_space=pltpu.SMEM)
VMEM = pl.BlockSpec(memory_space=pltpu.VMEM)


def exponent_rows():
    listing = []
    for degree in range(5):
        for power_x in range(degree, -1, -1):
            for power_y in range(degree - power_x, -1, -1):
                listing.append((power_x, power_y, degree - power_x - power_y))
    return listing


TRIPLES = exponent_rows()
SPOT = {triple: number for number, triple in enumerate(TRIPLES)}
AXES = ((1, 0, 0), (0, 1, 0), (0, 0, 1))


def plus(*triples):
    return tuple(sum(parts) for parts in zip(*triples))


def lanes_of(ref, comp, b):
    return ref[comp : comp + 1, pl.ds(pl.multiple_of(b * BUCKET, BUCKET), BUCKET)]


def monomial_sums(offsets, mass):
    x, y, z = offsets
    known = {(0, 0, 0): mass}
    sums = []
    for triple in TRIPLES:
        if triple not in known:
            axis = next(a for a in range(3) if triple[a] > 0)
            lower = tuple(p - (1 if a == axis else 0) for a, p in enumerate(triple))
            known[triple] = known[lower] * offsets[axis]
        sums.append(jnp.sum(known[triple], axis=1, keepdims=True))
    return sums


def cell_columns(moments, center):
    m = {triple: moments[number] for number, triple in enumerate(TRIPLES)}
    trace1 = [sum(m[plus(e, f, f)] for f in AXES) for e in AXES]
    pairs = [t for t in TRIPLES if sum(t) == 2]
    trace2 = [sum(m[plus(t, f, f)] for f in AXES) for t in pairs]
    full = trace2[0] + trace2[3] + trace2[5]
    scale = (1.0, 1.0, 1.5, 2.5, 4.375)
    columns = [m[t] * scale[sum(t)] for t in TRIPLES]
    columns += center
    columns += [-0.5 * (m[(2, 0, 0)] + m[(0, 2, 0)] + m[(0, 0, 2)])]
    columns += [1.5 * t for t in trace1]
    columns += [3.75 * t for t in trace2]
    columns += [0.375 * full]
    return columns


def spread(columns, lane):
    table = jnp.zeros(lane.shape, F32)
    for number, column in enumerate(columns):
        table = jnp.where(lane == number, column, table)
    return table


def pack_kernel(
    ids_ref,
    cell_ids_ref,
    parent_ref,
    pcent_ref,
    pos_ref,
    mass_ref,
    tiles_ref,
    first_ref,
    second_ref,
    rows,
    about,
    terms,
    cells,
    contrib,
):
    chips = first_ref.shape[0]
    for b in range(NB):
        at = pl.ds(b * BUCKET, BUCKET)
        for comp in range(4):
            row = pos_ref[comp : comp + 1, at] if comp < 3 else mass_ref[0:1, at]
            rows[comp, b : b + 1, :] = row
            tiles_ref[b, 2 * comp : 2 * comp + 1, :] = row[:, :128]
            tiles_ref[b, 2 * comp + 1 : 2 * comp + 2, :] = row[:, 128:]
        parent = parent_ref[b]
        for comp in range(3):
            about[comp, b : b + 1, :] = jnp.full((1, 128), pcent_ref[comp, parent], F32)
    lane = lax.broadcasted_iota(jnp.int32, (NB, 128), 1)

    coords = [rows[comp] for comp in range(3)]
    centers = [jnp.sum(c, axis=1, keepdims=True) * (1.0 / BUCKET) for c in coords]
    sums = monomial_sums([c - o for c, o in zip(coords, centers)], rows[3])
    cells[...] = spread(cell_columns(sums, centers), lane - CELL_LANE)
    parents = [about[comp, :, 0:1] for comp in range(3)]
    sums = monomial_sums([c - o for c, o in zip(coords, parents)], rows[3])
    terms[0] = spread(sums, lane)
    terms[1] = pltpu.roll(terms[0], 35, 1)
    contrib[...] = jnp.zeros(contrib.shape, F32)
    for b in range(NB):
        parent = parent_ref[b]
        row = pl.ds(((parent >> 4) << 3) + (parent & 7), 1)
        contrib[row, :] = contrib[row, :] + terms[(parent >> 3) & 1, b : b + 1, :]

    def fill(step, carry):
        for part in range(4):
            dest = step * 4 + part
            for slot in range(RQ):
                tile = tiles_ref[jnp.maximum(ids_ref[slot, dest], 0)]
                if slot < EARLY:
                    first_ref[dest, slot] = tile
                else:
                    second_ref[dest, slot - EARLY] = tile
            for slot in range(RQC):
                cell = cells[pl.ds(jnp.maximum(cell_ids_ref[slot, dest], 0), 1), :]
                first_ref[dest, EARLY, slot : slot + 1, :] = cell
            own = contrib[pl.ds(pl.multiple_of(dest * 8, 8), 8), :]
            first_ref[dest, EARLY] = first_ref[dest, EARLY] + own
        return carry

    lax.fori_loop(0, chips // 4, fill, 0)


def spread_group(tile_ref, number, spread_ref):
    for r in range(8):
        row = tile_ref[number, r : r + 1, :]
        spread_ref[r] = jnp.transpose(jnp.broadcast_to(row, (128, 128)))


def add_pair(spread_ref, targets, sums, row):
    tx, ty, tz = load_targets(targets, jnp.minimum(row >> 5, 1), row & 31)
    ax, ay, az = [sums[row, comp] for comp in range(3)]
    for h in range(2):
        for g in range(16):
            at = slice(8 * g, 8 * g + 8)
            sx, sy, sz, sm = [spread_ref[2 * comp + h, at, :] for comp in range(4)]
            sx, sy, sz, sm = [jnp.concatenate([v, v], axis=1) for v in (sx, sy, sz, sm)]
            dx = sx - tx
            dy = sy - ty
            dz = sz - tz
            inv = lax.rsqrt(dx * dx + dy * dy + (dz * dz + SOFT_SQ))
            weight = sm * inv * (inv * inv)
            ax = ax + weight * dx
            ay = ay + weight * dy
            az = az + weight * dz
    for comp, value in enumerate((ax, ay, az)):
        sums[row, comp] = value


def list_active(sub, act_ref, order):
    total = 0
    for row in range(2 * NB):
        listed = (sub if row < NB else 1 - sub) * NB + row % NB
        order[total] = row
        total = total + act_ref[listed]
    return total


def listed_row(sub, row):
    return row ^ (sub << 5)


def start_sums(order, total, sums, note, carry):
    def step(n, carry):
        row = order[n]
        for comp in range(3):
            sums[row, comp] = jnp.zeros((8, BUCKET), F32)
        return note(row, carry)

    return lax.fori_loop(0, total, step, carry)


def end_sums(order, total, sums, out_ref):
    def step(n, carry):
        row = order[n]
        add_rows(out_ref, row >> 5, row & 31, [sums[row, comp] for comp in range(3)])
        return carry

    lax.fori_loop(0, total, step, 0)


def load_targets(targets, half, b):
    return [
        jnp.broadcast_to(lanes_of(targets.at[half], comp, b), (8, BUCKET)) for comp in range(3)
    ]


def add_rows(ref, half, b, values):
    at = pl.ds(pl.multiple_of(b * BUCKET, BUCKET), BUCKET)
    for comp in range(3):
        row = jnp.sum(values[comp], axis=0, keepdims=True)
        ref[half, comp : comp + 1, at] = ref[half, comp : comp + 1, at] + row


def local_kernel(
    sub_ref, act_ref, list_ref, pos_ref, other_ref, tiles_ref, out_ref, targets, order, sums,
    one, two, users, counts,
):
    sub = sub_ref[0]
    targets[0] = pos_ref[...]
    targets[1] = other_ref[...]
    out_ref[...] = jnp.zeros(out_ref.shape, F32)
    for comp in range(3):
        sums[2 * NB, comp] = jnp.zeros((8, BUCKET), F32)
    for b in range(NB + 1):
        counts[b] = 0
        users[b * USES] = 2 * NB
    total = list_active(sub, act_ref, order)

    def note(row, carry):
        listed = listed_row(sub, row)
        for k in range(8):
            entry = list_ref[k, listed]
            group = jnp.where((entry >> 5) == sub, entry & 31, NB)
            count = counts[group]
            users[(group << USES_BITS) + count] = row
            counts[group] = count + 1
        return carry

    start_sums(order, total, sums, note, 0)

    def work(group, now, later):
        spread_group(tiles_ref, jnp.minimum(group + 1, NB - 1), later)
        first = group << USES_BITS
        add_pair(now, targets, sums, users[first])

        def more(use, carry):
            add_pair(now, targets, sums, users[first + use])
            return carry

        lax.fori_loop(1, counts[group], more, 0)

    spread_group(tiles_ref, 0, one)

    def step(pair, carry):
        work(2 * pair, one, two)
        work(2 * pair + 1, two, one)
        return carry

    lax.fori_loop(0, NB // 2, step, 0)
    end_sums(order, total, sums, out_ref)


def near_pairs(base, width, stride, sub, total, list_ref, pool_ref, out_ref, scratch):
    targets, order, sums, one, two, names, homes = scratch

    def note(row, count):
        listed = listed_row(sub, row)
        for k in range(8):
            entry = list_ref[k, listed]
            slot = (entry & (RQ - 1)) - base
            names[count] = (entry >> 3) * stride + slot
            homes[count] = row
            mine = (((entry >> 2) & 1) == sub) & (slot >= 0) & (slot < width)
            count = count + jnp.where(mine, 1, 0)
        return count

    count = start_sums(order, total, sums, note, jnp.int32(0))

    @pl.when(count > 0)
    def _():
        spread_group(pool_ref, names[0], one)

        def step(pair, carry):
            spread_group(pool_ref, names[2 * pair + 1], two)
            add_pair(one, targets, sums, homes[2 * pair])
            spread_group(pool_ref, names[jnp.minimum(2 * pair + 2, count - 1)], one)
            add_pair(two, targets, sums, homes[2 * pair + 1])
            return carry

        lax.fori_loop(0, count >> 1, step, 0)

        @pl.when((count & 1) == 1)
        def _():
            add_pair(one, targets, sums, homes[count - 1])

    end_sums(order, total, sums, out_ref)


def late_kernel(
    sub_ref, act_ref, list_ref, pos_ref, other_ref, pool_ref, part_ref, out_ref, targets, order,
    sums, one, two, names, homes,
):
    sub = sub_ref[0]
    targets[0] = pos_ref[...]
    targets[1] = other_ref[...]
    out_ref[...] = part_ref[...]
    total = list_active(sub, act_ref, order)
    scratch = (targets, order, sums, one, two, names, homes)
    wide = RQ - EARLY
    near_pairs(EARLY, wide, wide, sub, total, list_ref, pool_ref, out_ref, scratch)


def contract(tensor, axis, weighted):
    total = None
    for triple, value in weighted.items():
        term = tensor[plus(triple, AXES[axis])] * value
        total = term if total is None else total + term
    return total


def cell_pull(table, targets):
    def column(number):
        return table[:, CELL_LANE + number : CELL_LANE + number + 1]

    m = {triple: column(number) for number, triple in enumerate(TRIPLES)}
    r = [targets[a] - column(35 + a) for a in range(3)]
    x, y, z = r
    rho_sq = x * x + y * y + (z * z + FAR_SQ)
    inv = lax.rsqrt(rho_sq)
    inv_sq = inv * inv
    u = [inv]
    for _ in range(5):
        u.append(u[-1] * inv_sq)
    xx, yy, zz, xy, xz, yz = x * x, y * y, z * z, x * y, x * z, y * z
    first = {(1, 0, 0): x, (0, 1, 0): y, (0, 0, 1): z}
    second = {
        (2, 0, 0): xx,
        (1, 1, 0): 2.0 * xy,
        (1, 0, 1): 2.0 * xz,
        (0, 2, 0): yy,
        (0, 1, 1): 2.0 * yz,
        (0, 0, 2): zz,
    }
    x3, y3, z3 = 3.0 * x, 3.0 * y, 3.0 * z
    third = {
        (3, 0, 0): xx * x,
        (2, 1, 0): xx * y3,
        (2, 0, 1): xx * z3,
        (1, 2, 0): yy * x3,
        (1, 1, 1): xy * (2.0 * z3),
        (1, 0, 2): zz * x3,
        (0, 3, 0): yy * y,
        (0, 2, 1): yy * z3,
        (0, 1, 2): zz * y3,
        (0, 0, 3): zz * z,
    }
    pairs = [t for t in TRIPLES if sum(t) == 2]
    trace2 = {t: column(42 + number) for number, t in enumerate(pairs)}
    grad = []
    q1, q2, q3, q4 = column(38), column(48), None, None
    for a in range(3):
        m1 = m[AXES[a]]
        a2 = contract(m, a, first)
        b2 = column(39 + a)
        a3 = contract(m, a, second)
        b3 = contract(trace2, a, first)
        a4 = contract(m, a, third)
        grad.append(
            m1 * u[1]
            + (a2 + (a2 - b2)) * u[2]
            + (a3 + 2.0 * (a3 - b3)) * u[3]
            + (4.0 * a4) * u[4]
        )
        q1 = q1 + r[a] * m1
        q2 = q2 + r[a] * (a2 - b2)
        low, high = r[a] * (a3 - b3), r[a] * a4
        q3 = low if q3 is None else q3 + low
        q4 = high if q4 is None else q4 + high
    pull = (
        m[(0, 0, 0)] * u[1] + 3.0 * q1 * u[2] + 5.0 * q2 * u[3] + 7.0 * q3 * u[4] + 9.0 * q4 * u[5]
    )
    return [grad[a] - r[a] * pull for a in range(3)]


def far_cells(sub, total, list_ref, pool_ref, out_ref, targets, order, picked):
    place = lax.broadcasted_iota(jnp.int32, (8, 128), 0)

    def visit(n, carry):
        row = order[n]
        listed = listed_row(sub, row)
        count = 0
        for k in range(16):
            entry = list_ref[k, listed]
            at = pl.ds(count, 1)
            picked[at, :] = pool_ref[(entry >> 4) * (EARLY + 1) + EARLY, pl.ds(entry & (RQC - 1), 1), :]
            count = count + jnp.where(((entry >> 3) & 1) == sub, 1, 0)
        half, b = row >> 5, row & 31
        sides = load_targets(targets, half, b)

        def add_cells(step, sums):
            table = picked[pl.ds(pl.multiple_of(step * 8, 8), 8), :]
            table = jnp.where(place < count - step * 8, table, 0.0)
            return tuple(s + p for s, p in zip(sums, cell_pull(table, sides)))

        zero = jnp.zeros((8, BUCKET), F32)
        sums = lax.fori_loop(0, (count + 7) >> 3, add_cells, (zero, zero, zero))
        add_rows(out_ref, half, b, sums)
        return carry

    lax.fori_loop(0, total, visit, 0)


def early_kernel(
    sub_ref, act_ref, near_ref, far_ref, pos_ref, other_ref, pool_ref, part_ref, out_ref,
    owned_ref, targets, order, sums, one, two, names, homes, picked,
):
    sub = sub_ref[0]
    targets[0] = pos_ref[...]
    targets[1] = other_ref[...]
    out_ref[...] = part_ref[...]

    def gather_owned(step, total):
        for part in range(4):
            total = total + pool_ref[(step * 4 + part) * (EARLY + 1) + EARLY]
        return total

    chips = pool_ref.shape[0] // (EARLY + 1)
    owned_ref[...] = lax.fori_loop(0, chips // 4, gather_owned, jnp.zeros((8, 128), F32))
    total = list_active(sub, act_ref, order)
    far_cells(sub, total, far_ref, pool_ref, out_ref, targets, order, picked)
    scratch = (targets, order, sums, one, two, names, homes)
    near_pairs(0, EARLY, EARLY + 1, sub, total, near_ref, pool_ref, out_ref, scratch)


def finish_kernel(
    sub_ref, act_ref, part_ref, came_ref, old_ref, mom_ref, mom_came_ref, accel_ref, parent_ref
):
    sub = sub_ref[0]
    for b in range(NB):
        at = pl.ds(b * BUCKET, BUCKET)
        live = act_ref[sub * NB + b] > 0
        accel_ref[:, at] = jnp.where(live, part_ref[0, :, at] + came_ref[:, at], old_ref[:, at])
    both = mom_ref[...] + mom_came_ref[...]
    parent_ref[0:8, :] = both[:, 0:35]
    parent_ref[8:16, :] = both[:, 35:70]


def shape(*dims):
    return jax.ShapeDtypeStruct(dims, F32)


def local(
    positions,
    masses,
    old_accel,
    active,
    parent_of,
    parent_centers,
    local_list,
    near_list,
    far_list,
    send_ids,
    cell_send_ids,
):
    chips = lax.axis_size("dom")
    own = NB * BUCKET
    me = lax.axis_index("sub").astype(jnp.int32).reshape(1)
    swap = [(0, 1), (1, 0)]
    near_scratch = [
        pltpu.VMEM((2, 3, own), F32),
        pltpu.SMEM((2 * NB + 8,), jnp.int32),
        pltpu.VMEM((2 * NB + 1, 3, 8, BUCKET), F32),
        pltpu.VMEM((8, 128, 128), F32),
        pltpu.VMEM((8, 128, 128), F32),
    ]
    params = pltpu.CompilerParams(vmem_limit_bytes=32 << 20)

    other = lax.ppermute(positions, "sub", swap)

    tiles, first, second = pl.pallas_call(
        pack_kernel,
        in_specs=[SMEM, SMEM, SMEM, SMEM, VMEM, VMEM],
        out_specs=[VMEM, VMEM, VMEM],
        out_shape=[shape(NB, 8, 128), shape(chips, EARLY + 1, 8, 128), shape(chips, RQ - EARLY, 8, 128)],
        scratch_shapes=[
            pltpu.VMEM((4, NB, BUCKET), F32),
            pltpu.VMEM((3, NB, 128), F32),
            pltpu.VMEM((2, NB, 128), F32),
            pltpu.VMEM((NB, 128), F32),
            pltpu.VMEM((chips * 8, 128), F32),
        ],
        compiler_params=pltpu.CompilerParams(vmem_limit_bytes=60 << 20),
        name="pack",
    )(send_ids[0].T, cell_send_ids[0].T, parent_of, parent_centers, positions, masses.reshape(1, own))

    def exchange(blocks):
        flat = blocks.reshape(chips, -1, 128)
        came = lax.all_to_all(flat, "dom", split_axis=0, concat_axis=0, tiled=True)
        return came.reshape(blocks.shape)

    pool = exchange(first)

    part = pl.pallas_call(
        local_kernel,
        in_specs=[SMEM, SMEM, SMEM, VMEM, VMEM, VMEM],
        out_specs=VMEM,
        out_shape=shape(2, 3, own),
        scratch_shapes=near_scratch
        + [pltpu.SMEM(((NB + 1) * USES,), jnp.int32), pltpu.SMEM((NB + 1,), jnp.int32)],
        compiler_params=params,
        cost_estimate=pl.CostEstimate(flops=2 << 30, transcendentals=1 << 27, bytes_accessed=1 << 20),
        name="near_local",
    )(me, active, local_list.T, positions, other, tiles)

    pool, second, part = lax.optimization_barrier((pool, second, part))
    late_pool = exchange(second)

    pair_scratch = near_scratch + [pltpu.SMEM((USES + 8,), jnp.int32)] * 2
    part, owned = pl.pallas_call(
        early_kernel,
        in_specs=[SMEM, SMEM, SMEM, SMEM, VMEM, VMEM, VMEM, VMEM],
        out_specs=[VMEM, VMEM],
        out_shape=[shape(2, 3, own), shape(8, 128)],
        scratch_shapes=pair_scratch + [pltpu.VMEM((24, 128), F32)],
        compiler_params=params,
        cost_estimate=pl.CostEstimate(flops=2 << 30, transcendentals=1 << 27, bytes_accessed=1 << 20),
        name="early",
    )(me, active, near_list.T, far_list.T, positions, other, pool.reshape(-1, 8, 128), part)
    owned_came = lax.ppermute(owned, "sub", swap)
    part, owned_came = lax.optimization_barrier((part, owned_came))

    part = pl.pallas_call(
        late_kernel,
        in_specs=[SMEM, SMEM, SMEM, VMEM, VMEM, VMEM, VMEM],
        out_specs=VMEM,
        out_shape=shape(2, 3, own),
        scratch_shapes=pair_scratch,
        compiler_params=params,
        cost_estimate=pl.CostEstimate(flops=1 << 30, transcendentals=1 << 26, bytes_accessed=1 << 20),
        name="late",
    )(me, active, near_list.T, positions, other, late_pool.reshape(-1, 8, 128), part)

    came = lax.ppermute(part[1], "sub", swap)
    accel, parents = pl.pallas_call(
        finish_kernel,
        in_specs=[SMEM, SMEM, VMEM, VMEM, VMEM, VMEM, VMEM],
        out_specs=[VMEM, VMEM],
        out_shape=[shape(3, own), shape(16, 35)],
        compiler_params=params,
        name="finish",
    )(me, active, part, came, old_accel, owned, owned_came)
    return accel, parents.T


def solution(mesh):
    both = ("dom", "sub")
    in_specs = (
        P(None, both),
        P(both),
        P(None, both),
        P("dom"),
        P(both),
        P(),
        P("dom", None),
        P("dom", None),
        P("dom", None),
        P(both, None, None),
        P(both, None, None),
    )
    out_specs = (P(None, both), P(None, "dom"))
    return jax.shard_map(local, mesh=mesh, in_specs=in_specs, out_specs=out_specs, check_vma=False)
```

```python
import functools

import jax
import jax.numpy as jnp
from jax import lax
from jax.experimental import pallas as pl
from jax.experimental.pallas import tpu as pltpu
from jax.sharding import PartitionSpec as P

BUCKET = 256
NB = 32
RQ = 4
RQC = 8
CELL_LANE = 70
EARLY = 2
USES_BITS = 9
USES = 1 << USES_BITS
SOFT_SQ = 0.0025
FAR_SQ = 0.25
F32 = jnp.float32
SMEM = pl.BlockSpec(memory_space=pltpu.SMEM)
VMEM = pl.BlockSpec(memory_space=pltpu.VMEM)


def exponent_rows():
    listing = []
    for degree in range(5):
        for power_x in range(degree, -1, -1):
            for power_y in range(degree - power_x, -1, -1):
                listing.append((power_x, power_y, degree - power_x - power_y))
    return listing


TRIPLES = exponent_rows()
SPOT = {triple: number for number, triple in enumerate(TRIPLES)}
AXES = ((1, 0, 0), (0, 1, 0), (0, 0, 1))


def plus(*triples):
    return tuple(sum(parts) for parts in zip(*triples))


def lanes_of(ref, comp, b):
    return ref[comp : comp + 1, pl.ds(pl.multiple_of(b * BUCKET, BUCKET), BUCKET)]


def monomial_sums(offsets, mass):
    x, y, z = offsets
    known = {(0, 0, 0): mass}
    sums = []
    for triple in TRIPLES:
        if triple not in known:
            axis = next(a for a in range(3) if triple[a] > 0)
            lower = tuple(p - (1 if a == axis else 0) for a, p in enumerate(triple))
            known[triple] = known[lower] * offsets[axis]
        sums.append(jnp.sum(known[triple], axis=1, keepdims=True))
    return sums


def cell_columns(moments, center):
    m = {triple: moments[number] for number, triple in enumerate(TRIPLES)}
    trace1 = [sum(m[plus(e, f, f)] for f in AXES) for e in AXES]
    pairs = [t for t in TRIPLES if sum(t) == 2]
    trace2 = [sum(m[plus(t, f, f)] for f in AXES) for t in pairs]
    full = trace2[0] + trace2[3] + trace2[5]
    scale = (1.0, 1.0, 1.5, 2.5, 4.375)
    columns = [m[t] * scale[sum(t)] for t in TRIPLES]
    columns += center
    columns += [-0.5 * (m[(2, 0, 0)] + m[(0, 2, 0)] + m[(0, 0, 2)])]
    columns += [1.5 * t for t in trace1]
    columns += [3.75 * t for t in trace2]
    columns += [0.375 * full]
    return columns


def spread(columns, lane):
    table = jnp.zeros(lane.shape, F32)
    for number, column in enumerate(columns):
        table = jnp.where(lane == number, column, table)
    return table


def pack_kernel(
    ids_ref,
    cell_ids_ref,
    parent_ref,
    pcent_ref,
    pos_ref,
    mass_ref,
    tiles_ref,
    first_ref,
    second_ref,
    rows,
    about,
    terms,
    cells,
    contrib,
):
    chips = first_ref.shape[0]
    for b in range(NB):
        at = pl.ds(b * BUCKET, BUCKET)
        for comp in range(4):
            row = pos_ref[comp : comp + 1, at] if comp < 3 else mass_ref[0:1, at]
            rows[comp, b : b + 1, :] = row
            tiles_ref[b, 2 * comp : 2 * comp + 1, :] = row[:, :128]
            tiles_ref[b, 2 * comp + 1 : 2 * comp + 2, :] = row[:, 128:]
        parent = parent_ref[b]
        for comp in range(3):
            about[comp, b : b + 1, :] = jnp.full((1, 128), pcent_ref[comp, parent], F32)
    lane = lax.broadcasted_iota(jnp.int32, (NB, 128), 1)

    coords = [rows[comp] for comp in range(3)]
    centers = [jnp.sum(c, axis=1, keepdims=True) * (1.0 / BUCKET) for c in coords]
    sums = monomial_sums([c - o for c, o in zip(coords, centers)], rows[3])
    cells[...] = spread(cell_columns(sums, centers), lane - CELL_LANE)
    parents = [about[comp, :, 0:1] for comp in range(3)]
    sums = monomial_sums([c - o for c, o in zip(coords, parents)], rows[3])
    terms[0] = spread(sums, lane)
    terms[1] = pltpu.roll(terms[0], 35, 1)
    contrib[...] = jnp.zeros(contrib.shape, F32)
    for b in range(NB):
        parent = parent_ref[b]
        row = pl.ds(((parent >> 4) << 3) + (parent & 7), 1)
        contrib[row, :] = contrib[row, :] + terms[(parent >> 3) & 1, b : b + 1, :]

    def fill(step, carry):
        for part in range(4):
            dest = step * 4 + part
            for slot in range(RQ):
                tile = tiles_ref[jnp.maximum(ids_ref[slot, dest], 0)]
                if slot < EARLY:
                    first_ref[dest, slot] = tile
                else:
                    second_ref[dest, slot - EARLY] = tile
            for slot in range(RQC):
                cell = cells[pl.ds(jnp.maximum(cell_ids_ref[slot, dest], 0), 1), :]
                first_ref[dest, EARLY, slot : slot + 1, :] = cell
            own = contrib[pl.ds(pl.multiple_of(dest * 8, 8), 8), :]
            first_ref[dest, EARLY] = first_ref[dest, EARLY] + own
        return carry

    lax.fori_loop(0, chips // 4, fill, 0)


def spread_group(tile_ref, number, spread_ref):
    for r in range(8):
        row = tile_ref[number, r : r + 1, :]
        spread_ref[r] = jnp.transpose(jnp.broadcast_to(row, (128, 128)))


def add_pair(spread_ref, targets, sums, row):
    tx, ty, tz = load_targets(targets, jnp.minimum(row >> 5, 1), row & 31)
    ax, ay, az = [sums[row, comp] for comp in range(3)]
    for h in range(2):
        for g in range(16):
            at = slice(8 * g, 8 * g + 8)
            sx, sy, sz, sm = [spread_ref[2 * comp + h, at, :] for comp in range(4)]
            sx, sy, sz, sm = [jnp.concatenate([v, v], axis=1) for v in (sx, sy, sz, sm)]
            dx = sx - tx
            dy = sy - ty
            dz = sz - tz
            inv = lax.rsqrt(dx * dx + dy * dy + (dz * dz + SOFT_SQ))
            weight = sm * inv * (inv * inv)
            ax = ax + weight * dx
            ay = ay + weight * dy
            az = az + weight * dz
    for comp, value in enumerate((ax, ay, az)):
        sums[row, comp] = value


def list_active(sub, act_ref, order):
    total = 0
    for row in range(2 * NB):
        listed = (sub if row < NB else 1 - sub) * NB + row % NB
        order[total] = row
        total = total + act_ref[listed]
    return total


def listed_row(sub, row):
    return row ^ (sub << 5)


def start_sums(order, total, sums, note, carry):
    def step(n, carry):
        row = order[n]
        for comp in range(3):
            sums[row, comp] = jnp.zeros((8, BUCKET), F32)
        return note(row, carry)

    return lax.fori_loop(0, total, step, carry)


def end_sums(order, total, sums, out_ref):
    def step(n, carry):
        row = order[n]
        add_rows(out_ref, row >> 5, row & 31, [sums[row, comp] for comp in range(3)])
        return carry

    lax.fori_loop(0, total, step, 0)


def load_targets(targets, half, b):
    return [
        jnp.broadcast_to(lanes_of(targets.at[half], comp, b), (8, BUCKET)) for comp in range(3)
    ]


def add_rows(ref, half, b, values):
    at = pl.ds(pl.multiple_of(b * BUCKET, BUCKET), BUCKET)
    for comp in range(3):
        row = jnp.sum(values[comp], axis=0, keepdims=True)
        ref[half, comp : comp + 1, at] = ref[half, comp : comp + 1, at] + row


def local_kernel(
    sub_ref, act_ref, list_ref, pos_ref, other_ref, tiles_ref, out_ref, targets, order, sums,
    one, two, users, counts,
):
    sub = sub_ref[0]
    targets[0] = pos_ref[...]
    targets[1] = other_ref[...]
    out_ref[...] = jnp.zeros(out_ref.shape, F32)
    for comp in range(3):
        sums[2 * NB, comp] = jnp.zeros((8, BUCKET), F32)
    for b in range(NB + 1):
        counts[b] = 0
        users[b * USES] = 2 * NB
    total = list_active(sub, act_ref, order)

    def note(row, carry):
        listed = listed_row(sub, row)
        for k in range(8):
            entry = list_ref[k, listed]
            group = jnp.where((entry >> 5) == sub, entry & 31, NB)
            count = counts[group]
            users[(group << USES_BITS) + count] = row
            counts[group] = count + 1
        return carry

    start_sums(order, total, sums, note, 0)

    def work(group, now, later):
        spread_group(tiles_ref, jnp.minimum(group + 1, NB - 1), later)
        first = group << USES_BITS
        add_pair(now, targets, sums, users[first])

        def more(use, carry):
            add_pair(now, targets, sums, users[first + use])
            return carry

        lax.fori_loop(1, counts[group], more, 0)

    spread_group(tiles_ref, 0, one)

    def step(pair, carry):
        work(2 * pair, one, two)
        work(2 * pair + 1, two, one)
        return carry

    lax.fori_loop(0, NB // 2, step, 0)
    end_sums(order, total, sums, out_ref)


def near_pairs(base, width, stride, sub, total, list_ref, pool_ref, out_ref, scratch):
    targets, order, sums, one, two, names, homes = scratch

    def note(row, count):
        listed = listed_row(sub, row)
        for k in range(8):
            entry = list_ref[k, listed]
            slot = (entry & (RQ - 1)) - base
            names[count] = (entry >> 3) * stride + slot
            homes[count] = row
            mine = (((entry >> 2) & 1) == sub) & (slot >= 0) & (slot < width)
            count = count + jnp.where(mine, 1, 0)
        return count

    count = start_sums(order, total, sums, note, jnp.int32(0))

    @pl.when(count > 0)
    def _():
        spread_group(pool_ref, names[0], one)
        spread_group(pool_ref, names[jnp.minimum(1, count - 1)], two)

        def step(pair, carry):
            add_pair(one, targets, sums, homes[2 * pair])
            spread_group(pool_ref, names[jnp.minimum(2 * pair + 2, count - 1)], one)
            add_pair(two, targets, sums, homes[2 * pair + 1])
            spread_group(pool_ref, names[jnp.minimum(2 * pair + 3, count - 1)], two)
            return carry

        lax.fori_loop(0, count >> 1, step, 0)

        @pl.when((count & 1) == 1)
        def _():
            add_pair(one, targets, sums, homes[count - 1])

    end_sums(order, total, sums, out_ref)


def late_kernel(
    sub_ref, act_ref, list_ref, pos_ref, other_ref, pool_ref, part_ref, owned_ref, own_ref,
    send_ref, targets, order, sums, one, two, names, homes, both,
):
    sub = sub_ref[0]
    targets[0] = pos_ref[...]
    targets[1] = other_ref[...]
    both[...] = part_ref[...]
    total = list_active(sub, act_ref, order)
    scratch = (targets, order, sums, one, two, names, homes)
    wide = RQ - EARLY
    near_pairs(EARLY, wide, wide, sub, total, list_ref, pool_ref, both, scratch)
    own_ref[...] = both[0]
    send_ref[0:3, :] = both[1]
    send_ref[3:4, :] = jnp.zeros((1, send_ref.shape[1]), F32)
    for r in range(8):
        send_ref[3:4, 128 * r : 128 * r + 128] = owned_ref[r : r + 1, :]


def contract(tensor, axis, weighted):
    total = None
    for triple, value in weighted.items():
        term = tensor[plus(triple, AXES[axis])] * value
        total = term if total is None else total + term
    return total


def cell_pull(table, targets):
    def column(number):
        return table[:, CELL_LANE + number : CELL_LANE + number + 1]

    m = {triple: column(number) for number, triple in enumerate(TRIPLES)}
    r = [targets[a] - column(35 + a) for a in range(3)]
    x, y, z = r
    rho_sq = x * x + y * y + (z * z + FAR_SQ)
    inv = lax.rsqrt(rho_sq)
    inv_sq = inv * inv
    u = [inv]
    for _ in range(5):
        u.append(u[-1] * inv_sq)
    xx, yy, zz, xy, xz, yz = x * x, y * y, z * z, x * y, x * z, y * z
    first = {(1, 0, 0): x, (0, 1, 0): y, (0, 0, 1): z}
    second = {
        (2, 0, 0): xx,
        (1, 1, 0): 2.0 * xy,
        (1, 0, 1): 2.0 * xz,
        (0, 2, 0): yy,
        (0, 1, 1): 2.0 * yz,
        (0, 0, 2): zz,
    }
    x3, y3, z3 = 3.0 * x, 3.0 * y, 3.0 * z
    third = {
        (3, 0, 0): xx * x,
        (2, 1, 0): xx * y3,
        (2, 0, 1): xx * z3,
        (1, 2, 0): yy * x3,
        (1, 1, 1): xy * (2.0 * z3),
        (1, 0, 2): zz * x3,
        (0, 3, 0): yy * y,
        (0, 2, 1): yy * z3,
        (0, 1, 2): zz * y3,
        (0, 0, 3): zz * z,
    }
    pairs = [t for t in TRIPLES if sum(t) == 2]
    trace2 = {t: column(42 + number) for number, t in enumerate(pairs)}
    grad = []
    q1, q2, q3, q4 = column(38), column(48), None, None
    for a in range(3):
        m1 = m[AXES[a]]
        a2 = contract(m, a, first)
        b2 = column(39 + a)
        a3 = contract(m, a, second)
        b3 = contract(trace2, a, first)
        a4 = contract(m, a, third)
        grad.append(
            m1 * u[1]
            + (a2 + (a2 - b2)) * u[2]
            + (a3 + 2.0 * (a3 - b3)) * u[3]
            + (4.0 * a4) * u[4]
        )
        q1 = q1 + r[a] * m1
        q2 = q2 + r[a] * (a2 - b2)
        low, high = r[a] * (a3 - b3), r[a] * a4
        q3 = low if q3 is None else q3 + low
        q4 = high if q4 is None else q4 + high
    pull = (
        m[(0, 0, 0)] * u[1] + 3.0 * q1 * u[2] + 5.0 * q2 * u[3] + 7.0 * q3 * u[4] + 9.0 * q4 * u[5]
    )
    return [grad[a] - r[a] * pull for a in range(3)]


def far_cells(sub, total, list_ref, pool_ref, out_ref, targets, order, picked):
    place = lax.broadcasted_iota(jnp.int32, (8, 128), 0)

    def visit(n, carry):
        row = order[n]
        listed = listed_row(sub, row)
        count = 0
        for k in range(16):
            entry = list_ref[k, listed]
            at = pl.ds(count, 1)
            picked[at, :] = pool_ref[(entry >> 4) * (EARLY + 1) + EARLY, pl.ds(entry & (RQC - 1), 1), :]
            count = count + jnp.where(((entry >> 3) & 1) == sub, 1, 0)
        half, b = row >> 5, row & 31
        sides = load_targets(targets, half, b)

        def add_cells(step, sums):
            table = picked[pl.ds(pl.multiple_of(step * 8, 8), 8), :]
            table = jnp.where(place < count - step * 8, table, 0.0)
            return tuple(s + p for s, p in zip(sums, cell_pull(table, sides)))

        zero = jnp.zeros((8, BUCKET), F32)
        sums = lax.fori_loop(0, (count + 7) >> 3, add_cells, (zero, zero, zero))
        add_rows(out_ref, half, b, sums)
        return carry

    lax.fori_loop(0, total, visit, 0)


def early_kernel(
    sub_ref, act_ref, near_ref, far_ref, pos_ref, other_ref, pool_ref, part_ref, out_ref,
    owned_ref, targets, order, sums, one, two, names, homes, picked,
):
    sub = sub_ref[0]
    targets[0] = pos_ref[...]
    targets[1] = other_ref[...]
    out_ref[...] = part_ref[...]

    def gather_owned(step, total):
        for part in range(4):
            total = total + pool_ref[(step * 4 + part) * (EARLY + 1) + EARLY]
        return total

    chips = pool_ref.shape[0] // (EARLY + 1)
    owned_ref[...] = lax.fori_loop(0, chips // 4, gather_owned, jnp.zeros((8, 128), F32))
    total = list_active(sub, act_ref, order)
    far_cells(sub, total, far_ref, pool_ref, out_ref, targets, order, picked)
    scratch = (targets, order, sums, one, two, names, homes)
    near_pairs(0, EARLY, EARLY + 1, sub, total, near_ref, pool_ref, out_ref, scratch)


def finish_kernel(sub_ref, act_ref, part_ref, came_ref, old_ref, owned_ref, accel_ref, parent_ref):
    sub = sub_ref[0]
    for b in range(NB):
        at = pl.ds(b * BUCKET, BUCKET)
        live = act_ref[sub * NB + b] > 0
        accel_ref[:, at] = jnp.where(live, part_ref[:, at] + came_ref[0:3, at], old_ref[:, at])
    for r in range(8):
        row = owned_ref[r : r + 1, :] + came_ref[3:4, 128 * r : 128 * r + 128]
        parent_ref[r : r + 1, :] = row[:, 0:35]
        parent_ref[8 + r : 9 + r, :] = row[:, 35:70]


def shape(*dims):
    return jax.ShapeDtypeStruct(dims, F32)


def local(
    positions,
    masses,
    old_accel,
    active,
    parent_of,
    parent_centers,
    local_list,
    near_list,
    far_list,
    send_ids,
    cell_send_ids,
):
    chips = lax.axis_size("dom")
    own = NB * BUCKET
    me = lax.axis_index("sub").astype(jnp.int32).reshape(1)
    swap = [(0, 1), (1, 0)]
    near_scratch = [
        pltpu.VMEM((2, 3, own), F32),
        pltpu.SMEM((2 * NB + 8,), jnp.int32),
        pltpu.VMEM((2 * NB + 1, 3, 8, BUCKET), F32),
        pltpu.VMEM((8, 128, 128), F32),
        pltpu.VMEM((8, 128, 128), F32),
    ]
    params = pltpu.CompilerParams(vmem_limit_bytes=32 << 20)

    other = lax.ppermute(positions, "sub", swap)

    tiles, first, second = pl.pallas_call(
        pack_kernel,
        in_specs=[SMEM, SMEM, SMEM, SMEM, VMEM, VMEM],
        out_specs=[VMEM, VMEM, VMEM],
        out_shape=[shape(NB, 8, 128), shape(chips, EARLY + 1, 8, 128), shape(chips, RQ - EARLY, 8, 128)],
        scratch_shapes=[
            pltpu.VMEM((4, NB, BUCKET), F32),
            pltpu.VMEM((3, NB, 128), F32),
            pltpu.VMEM((2, NB, 128), F32),
            pltpu.VMEM((NB, 128), F32),
            pltpu.VMEM((chips * 8, 128), F32),
        ],
        compiler_params=pltpu.CompilerParams(vmem_limit_bytes=60 << 20),
        name="pack",
    )(send_ids[0].T, cell_send_ids[0].T, parent_of, parent_centers, positions, masses.reshape(1, own))

    def exchange(blocks):
        flat = blocks.reshape(chips, -1, 128)
        came = lax.all_to_all(flat, "dom", split_axis=0, concat_axis=0, tiled=True)
        return came.reshape(blocks.shape)

    pool = exchange(first)

    part = pl.pallas_call(
        local_kernel,
        in_specs=[SMEM, SMEM, SMEM, VMEM, VMEM, VMEM],
        out_specs=VMEM,
        out_shape=shape(2, 3, own),
        scratch_shapes=near_scratch
        + [pltpu.SMEM(((NB + 1) * USES,), jnp.int32), pltpu.SMEM((NB + 1,), jnp.int32)],
        compiler_params=params,
        cost_estimate=pl.CostEstimate(flops=2 << 30, transcendentals=1 << 27, bytes_accessed=1 << 20),
        name="near_local",
    )(me, active, local_list.T, positions, other, tiles)

    pool, second, part = lax.optimization_barrier((pool, second, part))
    late_pool = exchange(second)

    pair_scratch = near_scratch + [pltpu.SMEM((USES + 8,), jnp.int32)] * 2
    part, owned = pl.pallas_call(
        early_kernel,
        in_specs=[SMEM, SMEM, SMEM, SMEM, VMEM, VMEM, VMEM, VMEM],
        out_specs=[VMEM, VMEM],
        out_shape=[shape(2, 3, own), shape(8, 128)],
        scratch_shapes=pair_scratch + [pltpu.VMEM((24, 128), F32)],
        compiler_params=params,
        cost_estimate=pl.CostEstimate(flops=2 << 30, transcendentals=1 << 27, bytes_accessed=1 << 20),
        name="early",
    )(me, active, near_list.T, far_list.T, positions, other, pool.reshape(-1, 8, 128), part)
    part, send = pl.pallas_call(
        late_kernel,
        in_specs=[SMEM, SMEM, SMEM, VMEM, VMEM, VMEM, VMEM, VMEM],
        out_specs=[VMEM, VMEM],
        out_shape=[shape(3, own), shape(4, own)],
        scratch_shapes=pair_scratch + [pltpu.VMEM((2, 3, own), F32)],
        compiler_params=params,
        cost_estimate=pl.CostEstimate(flops=1 << 30, transcendentals=1 << 26, bytes_accessed=1 << 20),
        name="late",
    )(me, active, near_list.T, positions, other, late_pool.reshape(-1, 8, 128), part, owned)

    came = lax.ppermute(send, "sub", swap)
    accel, parents = pl.pallas_call(
        finish_kernel,
        in_specs=[SMEM, SMEM, VMEM, VMEM, VMEM, VMEM],
        out_specs=[VMEM, VMEM],
        out_shape=[shape(3, own), shape(16, 35)],
        compiler_params=params,
        name="finish",
    )(me, active, part, came, old_accel, owned)
    return accel, parents.T


def solution(mesh):
    both = ("dom", "sub")
    in_specs = (
        P(None, both),
        P(both),
        P(None, both),
        P("dom"),
        P(both),
        P(),
        P("dom", None),
        P("dom", None),
        P("dom", None),
        P(both, None, None),
        P(both, None, None),
    )
    out_specs = (P(None, both), P(None, "dom"))
    return jax.shard_map(local, mesh=mesh, in_specs=in_specs, out_specs=out_specs, check_vma=False)
```

```python
import functools

import jax
import jax.numpy as jnp
from jax import lax
from jax.experimental import pallas as pl
from jax.experimental.pallas import tpu as pltpu
from jax.sharding import PartitionSpec as P

BUCKET = 256
NB = 32
RQ = 4
RQC = 8
CELL_LANE = 70
EARLY = 2
USES_BITS = 9
USES = 1 << USES_BITS
SPAN = USES + 16
SOFT_SQ = 0.0025
FAR_SQ = 0.25
F32 = jnp.float32
SMEM = pl.BlockSpec(memory_space=pltpu.SMEM)
VMEM = pl.BlockSpec(memory_space=pltpu.VMEM)


def exponent_rows():
    listing = []
    for degree in range(5):
        for power_x in range(degree, -1, -1):
            for power_y in range(degree - power_x, -1, -1):
                listing.append((power_x, power_y, degree - power_x - power_y))
    return listing


TRIPLES = exponent_rows()
SPOT = {triple: number for number, triple in enumerate(TRIPLES)}
AXES = ((1, 0, 0), (0, 1, 0), (0, 0, 1))


def plus(*triples):
    return tuple(sum(parts) for parts in zip(*triples))


def lanes_of(ref, comp, b):
    return ref[comp : comp + 1, pl.ds(pl.multiple_of(b * BUCKET, BUCKET), BUCKET)]


def monomial_sums(offsets, mass):
    x, y, z = offsets
    known = {(0, 0, 0): mass}
    sums = []
    for triple in TRIPLES:
        if triple not in known:
            axis = next(a for a in range(3) if triple[a] > 0)
            lower = tuple(p - (1 if a == axis else 0) for a, p in enumerate(triple))
            known[triple] = known[lower] * offsets[axis]
        sums.append(jnp.sum(known[triple], axis=1, keepdims=True))
    return sums


def cell_columns(moments, center):
    m = {triple: moments[number] for number, triple in enumerate(TRIPLES)}
    trace1 = [sum(m[plus(e, f, f)] for f in AXES) for e in AXES]
    pairs = [t for t in TRIPLES if sum(t) == 2]
    trace2 = [sum(m[plus(t, f, f)] for f in AXES) for t in pairs]
    full = trace2[0] + trace2[3] + trace2[5]
    scale = (1.0, 1.0, 1.5, 2.5, 4.375)
    columns = [m[t] * scale[sum(t)] for t in TRIPLES]
    columns += center
    columns += [-0.5 * (m[(2, 0, 0)] + m[(0, 2, 0)] + m[(0, 0, 2)])]
    columns += [1.5 * t for t in trace1]
    columns += [3.75 * t for t in trace2]
    columns += [0.375 * full]
    return columns


def spread(columns, lane):
    table = jnp.zeros(lane.shape, F32)
    for number, column in enumerate(columns):
        table = jnp.where(lane == number, column, table)
    return table


def pack_kernel(
    ids_ref,
    cell_ids_ref,
    parent_ref,
    pcent_ref,
    pos_ref,
    mass_ref,
    tiles_ref,
    first_ref,
    second_ref,
    rows,
    about,
    terms,
    cells,
    contrib,
):
    chips = first_ref.shape[0]
    for b in range(NB):
        at = pl.ds(b * BUCKET, BUCKET)
        for comp in range(4):
            row = pos_ref[comp : comp + 1, at] if comp < 3 else mass_ref[0:1, at]
            rows[comp, b : b + 1, :] = row
            tiles_ref[b, 2 * comp : 2 * comp + 1, :] = row[:, :128]
            tiles_ref[b, 2 * comp + 1 : 2 * comp + 2, :] = row[:, 128:]
        parent = parent_ref[b]
        for comp in range(3):
            about[comp, b : b + 1, :] = jnp.full((1, 128), pcent_ref[comp, parent], F32)
    lane = lax.broadcasted_iota(jnp.int32, (NB, 128), 1)

    coords = [rows[comp] for comp in range(3)]
    centers = [jnp.sum(c, axis=1, keepdims=True) * (1.0 / BUCKET) for c in coords]
    sums = monomial_sums([c - o for c, o in zip(coords, centers)], rows[3])
    cells[...] = spread(cell_columns(sums, centers), lane - CELL_LANE)
    parents = [about[comp, :, 0:1] for comp in range(3)]
    sums = monomial_sums([c - o for c, o in zip(coords, parents)], rows[3])
    terms[0] = spread(sums, lane)
    terms[1] = pltpu.roll(terms[0], 35, 1)
    contrib[...] = jnp.zeros(contrib.shape, F32)
    for b in range(NB):
        parent = parent_ref[b]
        row = pl.ds(((parent >> 4) << 3) + (parent & 7), 1)
        contrib[row, :] = contrib[row, :] + terms[(parent >> 3) & 1, b : b + 1, :]

    def fill(step, carry):
        for part in range(4):
            dest = step * 4 + part
            for slot in range(RQ):
                tile = tiles_ref[jnp.maximum(ids_ref[slot, dest], 0)]
                if slot < EARLY:
                    first_ref[dest, slot] = tile
                else:
                    second_ref[dest, slot - EARLY] = tile
            for slot in range(RQC):
                cell = cells[pl.ds(jnp.maximum(cell_ids_ref[slot, dest], 0), 1), :]
                first_ref[dest, EARLY, slot : slot + 1, :] = cell
            own = contrib[pl.ds(pl.multiple_of(dest * 8, 8), 8), :]
            first_ref[dest, EARLY] = first_ref[dest, EARLY] + own
        return carry

    lax.fori_loop(0, chips // 4, fill, 0)


def spread_group(tile_ref, number, spread_ref):
    for r in range(8):
        row = tile_ref[number, r : r + 1, :]
        spread_ref[r] = jnp.transpose(jnp.broadcast_to(row, (128, 128)))


def add_pair(spread_ref, targets, sums, row):
    tx, ty, tz = load_targets(targets, jnp.minimum(row >> 5, 1), row & 31)
    ax, ay, az = [sums[row, comp] for comp in range(3)]
    for h in range(2):
        for g in range(16):
            at = slice(8 * g, 8 * g + 8)
            sx, sy, sz, sm = [spread_ref[2 * comp + h, at, :] for comp in range(4)]
            sx, sy, sz, sm = [jnp.concatenate([v, v], axis=1) for v in (sx, sy, sz, sm)]
            dx = sx - tx
            dy = sy - ty
            dz = sz - tz
            inv = lax.rsqrt(dx * dx + dy * dy + (dz * dz + SOFT_SQ))
            weight = sm * inv * (inv * inv)
            ax = ax + weight * dx
            ay = ay + weight * dy
            az = az + weight * dz
    for comp, value in enumerate((ax, ay, az)):
        sums[row, comp] = value


def list_active(sub, act_ref, order):
    total = 0
    for row in range(2 * NB):
        listed = (sub if row < NB else 1 - sub) * NB + row % NB
        order[total] = row
        total = total + act_ref[listed]
    return total


def listed_row(sub, row):
    return row ^ (sub << 5)


def start_sums(order, total, sums, note, carry):
    def step(n, carry):
        row = order[n]
        for comp in range(3):
            sums[row, comp] = jnp.zeros((8, BUCKET), F32)
        return note(row, carry)

    return lax.fori_loop(0, total, step, carry)


def end_sums(order, total, sums, out_ref):
    def step(n, carry):
        row = order[n]
        add_rows(out_ref, row >> 5, row & 31, [sums[row, comp] for comp in range(3)])
        return carry

    lax.fori_loop(0, total, step, 0)


def load_targets(targets, half, b):
    return [
        jnp.broadcast_to(lanes_of(targets.at[half], comp, b), (8, BUCKET)) for comp in range(3)
    ]


def add_rows(ref, half, b, values):
    at = pl.ds(pl.multiple_of(b * BUCKET, BUCKET), BUCKET)
    for comp in range(3):
        row = jnp.sum(values[comp], axis=0, keepdims=True)
        ref[half, comp : comp + 1, at] = ref[half, comp : comp + 1, at] + row


def local_kernel(
    sub_ref, act_ref, list_ref, near_ref, pos_ref, other_ref, tiles_ref, out_ref, pairs_ref,
    targets, order, sums, one, two, users, counts,
):
    sub = sub_ref[0]
    targets[0] = pos_ref[...]
    targets[1] = other_ref[...]
    out_ref[...] = jnp.zeros(out_ref.shape, F32)
    for comp in range(3):
        sums[2 * NB, comp] = jnp.zeros((8, BUCKET), F32)
    for b in range(NB + 1):
        counts[b] = 0
        users[b * USES] = 2 * NB
    total = list_active(sub, act_ref, order)

    def note(row, carry):
        listed = listed_row(sub, row)
        for k in range(8):
            entry = list_ref[k, listed]
            group = jnp.where((entry >> 5) == sub, entry & 31, NB)
            count = counts[group]
            users[(group << USES_BITS) + count] = row
            counts[group] = count + 1
        early, late = carry
        for k in range(8):
            entry = near_ref[k, listed]
            slot = entry & (RQ - 1)
            mine = jnp.where(((entry >> 2) & 1) == sub, 1, 0)
            soon = jnp.where(slot < EARLY, mine, 0)
            pairs_ref[early] = (entry >> 3) * (EARLY + 1) + slot
            pairs_ref[SPAN + early] = row
            pairs_ref[2 * SPAN + late] = (entry >> 3) * (RQ - EARLY) + slot - EARLY
            pairs_ref[3 * SPAN + late] = row
            early = early + soon
            late = late + (mine - soon)
        return early, late

    early, late = start_sums(order, total, sums, note, (jnp.int32(0), jnp.int32(0)))
    pairs_ref[4 * SPAN] = early
    pairs_ref[4 * SPAN + 1] = late

    def work(group, now, later):
        spread_group(tiles_ref, jnp.minimum(group + 1, NB - 1), later)
        first = group << USES_BITS
        add_pair(now, targets, sums, users[first])

        def more(use, carry):
            add_pair(now, targets, sums, users[first + use])
            return carry

        lax.fori_loop(1, counts[group], more, 0)

    spread_group(tiles_ref, 0, one)

    def step(pair, carry):
        work(2 * pair, one, two)
        work(2 * pair + 1, two, one)
        return carry

    lax.fori_loop(0, NB // 2, step, 0)
    end_sums(order, total, sums, out_ref)


def near_pairs(part, total, pairs_ref, pool_ref, out_ref, scratch):
    targets, order, sums, one, two = scratch
    count = pairs_ref[4 * SPAN + part]

    def name(n):
        return pairs_ref[2 * part * SPAN + jnp.minimum(n, count - 1)]

    def home(n):
        return pairs_ref[(2 * part + 1) * SPAN + n]

    start_sums(order, total, sums, lambda row, carry: carry, 0)

    @pl.when(count > 0)
    def _():
        spread_group(pool_ref, name(0), one)
        spread_group(pool_ref, name(1), two)

        def step(pair, carry):
            add_pair(one, targets, sums, home(2 * pair))
            spread_group(pool_ref, name(2 * pair + 2), one)
            add_pair(two, targets, sums, home(2 * pair + 1))
            spread_group(pool_ref, name(2 * pair + 3), two)
            return carry

        lax.fori_loop(0, count >> 1, step, 0)

        @pl.when((count & 1) == 1)
        def _():
            add_pair(one, targets, sums, home(count - 1))

    end_sums(order, total, sums, out_ref)


def late_kernel(
    sub_ref, act_ref, pairs_ref, pos_ref, other_ref, pool_ref, part_ref, owned_ref, own_ref,
    send_ref, targets, order, sums, one, two, both,
):
    sub = sub_ref[0]
    targets[0] = pos_ref[...]
    targets[1] = other_ref[...]
    both[...] = part_ref[...]
    total = list_active(sub, act_ref, order)
    near_pairs(1, total, pairs_ref, pool_ref, both, (targets, order, sums, one, two))
    own_ref[...] = both[0]
    send_ref[0:3, :] = both[1]
    send_ref[3:4, :] = jnp.zeros((1, send_ref.shape[1]), F32)
    for r in range(8):
        send_ref[3:4, 128 * r : 128 * r + 128] = owned_ref[r : r + 1, :]


def contract(tensor, axis, weighted):
    total = None
    for triple, value in weighted.items():
        term = tensor[plus(triple, AXES[axis])] * value
        total = term if total is None else total + term
    return total


def cell_pull(table, targets):
    def column(number):
        return table[:, CELL_LANE + number : CELL_LANE + number + 1]

    m = {triple: column(number) for number, triple in enumerate(TRIPLES)}
    r = [targets[a] - column(35 + a) for a in range(3)]
    x, y, z = r
    rho_sq = x * x + y * y + (z * z + FAR_SQ)
    inv = lax.rsqrt(rho_sq)
    inv_sq = inv * inv
    u = [inv]
    for _ in range(5):
        u.append(u[-1] * inv_sq)
    xx, yy, zz, xy, xz, yz = x * x, y * y, z * z, x * y, x * z, y * z
    first = {(1, 0, 0): x, (0, 1, 0): y, (0, 0, 1): z}
    second = {
        (2, 0, 0): xx,
        (1, 1, 0): 2.0 * xy,
        (1, 0, 1): 2.0 * xz,
        (0, 2, 0): yy,
        (0, 1, 1): 2.0 * yz,
        (0, 0, 2): zz,
    }
    x3, y3, z3 = 3.0 * x, 3.0 * y, 3.0 * z
    third = {
        (3, 0, 0): xx * x,
        (2, 1, 0): xx * y3,
        (2, 0, 1): xx * z3,
        (1, 2, 0): yy * x3,
        (1, 1, 1): xy * (2.0 * z3),
        (1, 0, 2): zz * x3,
        (0, 3, 0): yy * y,
        (0, 2, 1): yy * z3,
        (0, 1, 2): zz * y3,
        (0, 0, 3): zz * z,
    }
    pairs = [t for t in TRIPLES if sum(t) == 2]
    trace2 = {t: column(42 + number) for number, t in enumerate(pairs)}
    grad = []
    q1, q2, q3, q4 = column(38), column(48), None, None
    for a in range(3):
        m1 = m[AXES[a]]
        a2 = contract(m, a, first)
        b2 = column(39 + a)
        a3 = contract(m, a, second)
        b3 = contract(trace2, a, first)
        a4 = contract(m, a, third)
        grad.append(
            m1 * u[1]
            + (a2 + (a2 - b2)) * u[2]
            + (a3 + 2.0 * (a3 - b3)) * u[3]
            + (4.0 * a4) * u[4]
        )
        q1 = q1 + r[a] * m1
        q2 = q2 + r[a] * (a2 - b2)
        low, high = r[a] * (a3 - b3), r[a] * a4
        q3 = low if q3 is None else q3 + low
        q4 = high if q4 is None else q4 + high
    pull = (
        m[(0, 0, 0)] * u[1] + 3.0 * q1 * u[2] + 5.0 * q2 * u[3] + 7.0 * q3 * u[4] + 9.0 * q4 * u[5]
    )
    return [grad[a] - r[a] * pull for a in range(3)]


def far_cells(sub, total, list_ref, pool_ref, out_ref, targets, order, picked):
    place = lax.broadcasted_iota(jnp.int32, (8, 128), 0)

    def visit(n, carry):
        row = order[n]
        listed = listed_row(sub, row)
        count = 0
        for k in range(16):
            entry = list_ref[k, listed]
            at = pl.ds(count, 1)
            picked[at, :] = pool_ref[(entry >> 4) * (EARLY + 1) + EARLY, pl.ds(entry & (RQC - 1), 1), :]
            count = count + jnp.where(((entry >> 3) & 1) == sub, 1, 0)
        half, b = row >> 5, row & 31
        sides = load_targets(targets, half, b)

        def add_cells(step, sums):
            table = picked[pl.ds(pl.multiple_of(step * 8, 8), 8), :]
            table = jnp.where(place < count - step * 8, table, 0.0)
            return tuple(s + p for s, p in zip(sums, cell_pull(table, sides)))

        zero = jnp.zeros((8, BUCKET), F32)
        sums = lax.fori_loop(0, (count + 7) >> 3, add_cells, (zero, zero, zero))
        add_rows(out_ref, half, b, sums)
        return carry

    lax.fori_loop(0, total, visit, 0)


def early_kernel(
    sub_ref, act_ref, pairs_ref, far_ref, pos_ref, other_ref, pool_ref, part_ref, out_ref,
    owned_ref, targets, order, sums, one, two, picked,
):
    sub = sub_ref[0]
    targets[0] = pos_ref[...]
    targets[1] = other_ref[...]
    out_ref[...] = part_ref[...]

    def gather_owned(step, total):
        for part in range(4):
            total = total + pool_ref[(step * 4 + part) * (EARLY + 1) + EARLY]
        return total

    chips = pool_ref.shape[0] // (EARLY + 1)
    owned_ref[...] = lax.fori_loop(0, chips // 4, gather_owned, jnp.zeros((8, 128), F32))
    total = list_active(sub, act_ref, order)
    far_cells(sub, total, far_ref, pool_ref, out_ref, targets, order, picked)
    near_pairs(0, total, pairs_ref, pool_ref, out_ref, (targets, order, sums, one, two))


def finish_kernel(sub_ref, act_ref, part_ref, came_ref, old_ref, owned_ref, accel_ref, parent_ref):
    sub = sub_ref[0]
    for b in range(NB):
        at = pl.ds(b * BUCKET, BUCKET)
        live = act_ref[sub * NB + b] > 0
        accel_ref[:, at] = jnp.where(live, part_ref[:, at] + came_ref[0:3, at], old_ref[:, at])
    for r in range(8):
        row = owned_ref[r : r + 1, :] + came_ref[3:4, 128 * r : 128 * r + 128]
        parent_ref[r : r + 1, :] = row[:, 0:35]
        parent_ref[8 + r : 9 + r, :] = row[:, 35:70]


def shape(*dims):
    return jax.ShapeDtypeStruct(dims, F32)


def local(
    positions,
    masses,
    old_accel,
    active,
    parent_of,
    parent_centers,
    local_list,
    near_list,
    far_list,
    send_ids,
    cell_send_ids,
):
    chips = lax.axis_size("dom")
    own = NB * BUCKET
    me = lax.axis_index("sub").astype(jnp.int32).reshape(1)
    swap = [(0, 1), (1, 0)]
    near_scratch = [
        pltpu.VMEM((2, 3, own), F32),
        pltpu.SMEM((2 * NB + 8,), jnp.int32),
        pltpu.VMEM((2 * NB + 1, 3, 8, BUCKET), F32),
        pltpu.VMEM((8, 128, 128), F32),
        pltpu.VMEM((8, 128, 128), F32),
    ]
    params = pltpu.CompilerParams(vmem_limit_bytes=32 << 20)

    other = lax.ppermute(positions, "sub", swap)

    tiles, first, second = pl.pallas_call(
        pack_kernel,
        in_specs=[SMEM, SMEM, SMEM, SMEM, VMEM, VMEM],
        out_specs=[VMEM, VMEM, VMEM],
        out_shape=[shape(NB, 8, 128), shape(chips, EARLY + 1, 8, 128), shape(chips, RQ - EARLY, 8, 128)],
        scratch_shapes=[
            pltpu.VMEM((4, NB, BUCKET), F32),
            pltpu.VMEM((3, NB, 128), F32),
            pltpu.VMEM((2, NB, 128), F32),
            pltpu.VMEM((NB, 128), F32),
            pltpu.VMEM((chips * 8, 128), F32),
        ],
        compiler_params=pltpu.CompilerParams(vmem_limit_bytes=60 << 20),
        name="pack",
    )(send_ids[0].T, cell_send_ids[0].T, parent_of, parent_centers, positions, masses.reshape(1, own))

    def exchange(blocks):
        flat = blocks.reshape(chips, -1, 128)
        came = lax.all_to_all(flat, "dom", split_axis=0, concat_axis=0, tiled=True)
        return came.reshape(blocks.shape)

    pool = exchange(first)

    part, pairs = pl.pallas_call(
        local_kernel,
        in_specs=[SMEM, SMEM, SMEM, SMEM, VMEM, VMEM, VMEM],
        out_specs=[VMEM, SMEM],
        out_shape=[shape(2, 3, own), jax.ShapeDtypeStruct((4 * SPAN + 16,), jnp.int32)],
        scratch_shapes=near_scratch
        + [pltpu.SMEM(((NB + 1) * USES,), jnp.int32), pltpu.SMEM((NB + 1,), jnp.int32)],
        compiler_params=params,
        cost_estimate=pl.CostEstimate(flops=2 << 30, transcendentals=1 << 27, bytes_accessed=1 << 20),
        name="near_local",
    )(me, active, local_list.T, near_list.T, positions, other, tiles)

    pool, second, part = lax.optimization_barrier((pool, second, part))
    late_pool = exchange(second)

    part, owned = pl.pallas_call(
        early_kernel,
        in_specs=[SMEM, SMEM, SMEM, SMEM, VMEM, VMEM, VMEM, VMEM],
        out_specs=[VMEM, VMEM],
        out_shape=[shape(2, 3, own), shape(8, 128)],
        scratch_shapes=near_scratch + [pltpu.VMEM((24, 128), F32)],
        compiler_params=params,
        cost_estimate=pl.CostEstimate(flops=2 << 30, transcendentals=1 << 27, bytes_accessed=1 << 20),
        name="early",
    )(me, active, pairs, far_list.T, positions, other, pool.reshape(-1, 8, 128), part)
    part, send = pl.pallas_call(
        late_kernel,
        in_specs=[SMEM, SMEM, SMEM, VMEM, VMEM, VMEM, VMEM, VMEM],
        out_specs=[VMEM, VMEM],
        out_shape=[shape(3, own), shape(4, own)],
        scratch_shapes=near_scratch + [pltpu.VMEM((2, 3, own), F32)],
        compiler_params=params,
        cost_estimate=pl.CostEstimate(flops=1 << 30, transcendentals=1 << 26, bytes_accessed=1 << 20),
        name="late",
    )(me, active, pairs, positions, other, late_pool.reshape(-1, 8, 128), part, owned)

    came = lax.ppermute(send, "sub", swap)
    accel, parents = pl.pallas_call(
        finish_kernel,
        in_specs=[SMEM, SMEM, VMEM, VMEM, VMEM, VMEM],
        out_specs=[VMEM, VMEM],
        out_shape=[shape(3, own), shape(16, 35)],
        compiler_params=params,
        name="finish",
    )(me, active, part, came, old_accel, owned)
    return accel, parents.T


def solution(mesh):
    both = ("dom", "sub")
    in_specs = (
        P(None, both),
        P(both),
        P(None, both),
        P("dom"),
        P(both),
        P(),
        P("dom", None),
        P("dom", None),
        P("dom", None),
        P(both, None, None),
        P(both, None, None),
    )
    out_specs = (P(None, both), P(None, "dom"))
    return jax.shard_map(local, mesh=mesh, in_specs=in_specs, out_specs=out_specs, check_vma=False)
```

```python
import functools

import jax
import jax.numpy as jnp
from jax import lax
from jax.experimental import pallas as pl
from jax.experimental.pallas import tpu as pltpu
from jax.sharding import PartitionSpec as P

BUCKET = 256
NB = 32
RQ = 4
RQC = 8
CELL_LANE = 70
EARLY = 2
USES_BITS = 9
USES = 1 << USES_BITS
SPAN = USES + 16
SOFT_SQ = 0.0025
FAR_SQ = 0.25
F32 = jnp.float32
SMEM = pl.BlockSpec(memory_space=pltpu.SMEM)
VMEM = pl.BlockSpec(memory_space=pltpu.VMEM)


def exponent_rows():
    listing = []
    for degree in range(5):
        for power_x in range(degree, -1, -1):
            for power_y in range(degree - power_x, -1, -1):
                listing.append((power_x, power_y, degree - power_x - power_y))
    return listing


TRIPLES = exponent_rows()
SPOT = {triple: number for number, triple in enumerate(TRIPLES)}
AXES = ((1, 0, 0), (0, 1, 0), (0, 0, 1))


def plus(*triples):
    return tuple(sum(parts) for parts in zip(*triples))


def lanes_of(ref, comp, b):
    return ref[comp : comp + 1, pl.ds(pl.multiple_of(b * BUCKET, BUCKET), BUCKET)]


def pack_late_kernel(ids_ref, tiles_ref, second_ref):
    def fill(step, carry):
        for part in range(4):
            dest = step * 4 + part
            for slot in range(EARLY, RQ):
                group = jnp.maximum(ids_ref[slot, dest], 0)
                second_ref[dest, slot - EARLY] = tiles_ref[group]
        return carry

    lax.fori_loop(0, second_ref.shape[0] // 4, fill, 0)


def monomial_sums(offsets, mass):
    x, y, z = offsets
    known = {(0, 0, 0): mass}
    sums = []
    for triple in TRIPLES:
        if triple not in known:
            axis = next(a for a in range(3) if triple[a] > 0)
            lower = tuple(p - (1 if a == axis else 0) for a, p in enumerate(triple))
            known[triple] = known[lower] * offsets[axis]
        sums.append(jnp.sum(known[triple], axis=1, keepdims=True))
    return sums


def cell_columns(moments, center):
    m = {triple: moments[number] for number, triple in enumerate(TRIPLES)}
    trace1 = [sum(m[plus(e, f, f)] for f in AXES) for e in AXES]
    pairs = [t for t in TRIPLES if sum(t) == 2]
    trace2 = [sum(m[plus(t, f, f)] for f in AXES) for t in pairs]
    full = trace2[0] + trace2[3] + trace2[5]
    scale = (1.0, 1.0, 1.5, 2.5, 4.375)
    columns = [m[t] * scale[sum(t)] for t in TRIPLES]
    columns += center
    columns += [-0.5 * (m[(2, 0, 0)] + m[(0, 2, 0)] + m[(0, 0, 2)])]
    columns += [1.5 * t for t in trace1]
    columns += [3.75 * t for t in trace2]
    columns += [0.375 * full]
    return columns


def spread(columns, lane):
    table = jnp.zeros(lane.shape, F32)
    for number, column in enumerate(columns):
        table = jnp.where(lane == number, column, table)
    return table


def pack_kernel(
    ids_ref,
    cell_ids_ref,
    parent_ref,
    pcent_ref,
    pos_ref,
    mass_ref,
    tiles_ref,
    first_ref,
    rows,
    about,
    terms,
    cells,
    contrib,
):
    chips = first_ref.shape[0]
    for b in range(NB):
        at = pl.ds(b * BUCKET, BUCKET)
        for comp in range(4):
            row = pos_ref[comp : comp + 1, at] if comp < 3 else mass_ref[0:1, at]
            rows[comp, b : b + 1, :] = row
            tiles_ref[b, 2 * comp : 2 * comp + 1, :] = row[:, :128]
            tiles_ref[b, 2 * comp + 1 : 2 * comp + 2, :] = row[:, 128:]
        parent = parent_ref[b]
        for comp in range(3):
            about[comp, b : b + 1, :] = jnp.full((1, 128), pcent_ref[comp, parent], F32)
    lane = lax.broadcasted_iota(jnp.int32, (NB, 128), 1)

    coords = [rows[comp] for comp in range(3)]
    centers = [jnp.sum(c, axis=1, keepdims=True) * (1.0 / BUCKET) for c in coords]
    sums = monomial_sums([c - o for c, o in zip(coords, centers)], rows[3])
    cells[...] = spread(cell_columns(sums, centers), lane - CELL_LANE)
    parents = [about[comp, :, 0:1] for comp in range(3)]
    sums = monomial_sums([c - o for c, o in zip(coords, parents)], rows[3])
    terms[0] = spread(sums, lane)
    terms[1] = pltpu.roll(terms[0], 35, 1)
    contrib[...] = jnp.zeros(contrib.shape, F32)
    for b in range(NB):
        parent = parent_ref[b]
        row = pl.ds(((parent >> 4) << 3) + (parent & 7), 1)
        contrib[row, :] = contrib[row, :] + terms[(parent >> 3) & 1, b : b + 1, :]

    def fill(step, carry):
        for part in range(4):
            dest = step * 4 + part
            for slot in range(EARLY):
                first_ref[dest, slot] = tiles_ref[jnp.maximum(ids_ref[slot, dest], 0)]
            for slot in range(RQC):
                cell = cells[pl.ds(jnp.maximum(cell_ids_ref[slot, dest], 0), 1), :]
                first_ref[dest, EARLY, slot : slot + 1, :] = cell
            own = contrib[pl.ds(pl.multiple_of(dest * 8, 8), 8), :]
            first_ref[dest, EARLY] = first_ref[dest, EARLY] + own
        return carry

    lax.fori_loop(0, chips // 4, fill, 0)


def spread_group(tile_ref, number, spread_ref):
    for r in range(8):
        row = tile_ref[number, r : r + 1, :]
        spread_ref[r] = jnp.transpose(jnp.broadcast_to(row, (128, 128)))


def add_pair(spread_ref, targets, sums, row):
    tx, ty, tz = load_targets(targets, jnp.minimum(row >> 5, 1), row & 31)
    ax, ay, az = [sums[row, comp] for comp in range(3)]
    for h in range(2):
        for g in range(16):
            at = slice(8 * g, 8 * g + 8)
            sx, sy, sz, sm = [spread_ref[2 * comp + h, at, :] for comp in range(4)]
            sx, sy, sz, sm = [jnp.concatenate([v, v], axis=1) for v in (sx, sy, sz, sm)]
            dx = sx - tx
            dy = sy - ty
            dz = sz - tz
            inv = lax.rsqrt(dx * dx + dy * dy + (dz * dz + SOFT_SQ))
            weight = sm * inv * (inv * inv)
            ax = ax + weight * dx
            ay = ay + weight * dy
            az = az + weight * dz
    for comp, value in enumerate((ax, ay, az)):
        sums[row, comp] = value


def list_active(sub, act_ref, order):
    total = 0
    for row in range(2 * NB):
        listed = (sub if row < NB else 1 - sub) * NB + row % NB
        order[total] = row
        total = total + act_ref[listed]
    return total


def listed_row(sub, row):
    return row ^ (sub << 5)


def start_sums(order, total, sums, note, carry):
    def step(n, carry):
        row = order[n]
        for comp in range(3):
            sums[row, comp] = jnp.zeros((8, BUCKET), F32)
        return note(row, carry)

    return lax.fori_loop(0, total, step, carry)


def end_sums(order, total, sums, out_ref):
    def step(n, carry):
        row = order[n]
        add_rows(out_ref, row >> 5, row & 31, [sums[row, comp] for comp in range(3)])
        return carry

    lax.fori_loop(0, total, step, 0)


def load_targets(targets, half, b):
    return [
        jnp.broadcast_to(lanes_of(targets.at[half], comp, b), (8, BUCKET)) for comp in range(3)
    ]


def add_rows(ref, half, b, values):
    at = pl.ds(pl.multiple_of(b * BUCKET, BUCKET), BUCKET)
    for comp in range(3):
        row = jnp.sum(values[comp], axis=0, keepdims=True)
        ref[half, comp : comp + 1, at] = ref[half, comp : comp + 1, at] + row


def local_kernel(
    sub_ref, act_ref, list_ref, near_ref, pos_ref, other_ref, tiles_ref, out_ref, pairs_ref,
    targets, order, sums, one, two, users, counts,
):
    sub = sub_ref[0]
    targets[0] = pos_ref[...]
    targets[1] = other_ref[...]
    out_ref[...] = jnp.zeros(out_ref.shape, F32)
    for comp in range(3):
        sums[2 * NB, comp] = jnp.zeros((8, BUCKET), F32)
    for b in range(NB + 1):
        counts[b] = 0
        users[b * USES] = 2 * NB
    total = list_active(sub, act_ref, order)

    def note(row, carry):
        listed = listed_row(sub, row)
        for k in range(8):
            entry = list_ref[k, listed]
            group = jnp.where((entry >> 5) == sub, entry & 31, NB)
            count = counts[group]
            users[(group << USES_BITS) + count] = row
            counts[group] = count + 1
        early, late = carry
        for k in range(8):
            entry = near_ref[k, listed]
            slot = entry & (RQ - 1)
            mine = jnp.where(((entry >> 2) & 1) == sub, 1, 0)
            soon = jnp.where(slot < EARLY, mine, 0)
            pairs_ref[early] = (entry >> 3) * (EARLY + 1) + slot
            pairs_ref[SPAN + early] = row
            pairs_ref[2 * SPAN + late] = (entry >> 3) * (RQ - EARLY) + slot - EARLY
            pairs_ref[3 * SPAN + late] = row
            early = early + soon
            late = late + (mine - soon)
        return early, late

    early, late = start_sums(order, total, sums, note, (jnp.int32(0), jnp.int32(0)))
    pairs_ref[4 * SPAN] = early
    pairs_ref[4 * SPAN + 1] = late

    def work(group, now, later):
        spread_group(tiles_ref, jnp.minimum(group + 1, NB - 1), later)
        first = group << USES_BITS
        add_pair(now, targets, sums, users[first])

        def more(use, carry):
            add_pair(now, targets, sums, users[first + use])
            return carry

        lax.fori_loop(1, counts[group], more, 0)

    spread_group(tiles_ref, 0, one)

    def step(pair, carry):
        work(2 * pair, one, two)
        work(2 * pair + 1, two, one)
        return carry

    lax.fori_loop(0, NB // 2, step, 0)
    end_sums(order, total, sums, out_ref)


def near_pairs(part, total, pairs_ref, pool_ref, out_ref, scratch):
    targets, order, sums, one, two = scratch
    count = pairs_ref[4 * SPAN + part]

    def name(n):
        return pairs_ref[2 * part * SPAN + jnp.minimum(n, count - 1)]

    def home(n):
        return pairs_ref[(2 * part + 1) * SPAN + n]

    start_sums(order, total, sums, lambda row, carry: carry, 0)

    @pl.when(count > 0)
    def _():
        spread_group(pool_ref, name(0), one)
        spread_group(pool_ref, name(1), two)

        def step(pair, carry):
            add_pair(one, targets, sums, home(2 * pair))
            spread_group(pool_ref, name(2 * pair + 2), one)
            add_pair(two, targets, sums, home(2 * pair + 1))
            spread_group(pool_ref, name(2 * pair + 3), two)
            return carry

        lax.fori_loop(0, count >> 1, step, 0)

        @pl.when((count & 1) == 1)
        def _():
            add_pair(one, targets, sums, home(count - 1))

    end_sums(order, total, sums, out_ref)


def late_kernel(
    sub_ref, act_ref, pairs_ref, pos_ref, other_ref, pool_ref, part_ref, owned_ref, own_ref,
    send_ref, targets, order, sums, one, two, both,
):
    sub = sub_ref[0]
    targets[0] = pos_ref[...]
    targets[1] = other_ref[...]
    both[...] = part_ref[...]
    total = list_active(sub, act_ref, order)
    near_pairs(1, total, pairs_ref, pool_ref, both, (targets, order, sums, one, two))
    own_ref[...] = both[0]
    send_ref[0:3, :] = both[1]
    send_ref[3:4, :] = jnp.zeros((1, send_ref.shape[1]), F32)
    for r in range(8):
        send_ref[3:4, 128 * r : 128 * r + 128] = owned_ref[r : r + 1, :]


def contract(tensor, axis, weighted):
    total = None
    for triple, value in weighted.items():
        term = tensor[plus(triple, AXES[axis])] * value
        total = term if total is None else total + term
    return total


def cell_pull(table, targets):
    def column(number):
        return table[:, CELL_LANE + number : CELL_LANE + number + 1]

    m = {triple: column(number) for number, triple in enumerate(TRIPLES)}
    r = [targets[a] - column(35 + a) for a in range(3)]
    x, y, z = r
    rho_sq = x * x + y * y + (z * z + FAR_SQ)
    inv = lax.rsqrt(rho_sq)
    inv_sq = inv * inv
    u = [inv]
    for _ in range(5):
        u.append(u[-1] * inv_sq)
    xx, yy, zz, xy, xz, yz = x * x, y * y, z * z, x * y, x * z, y * z
    first = {(1, 0, 0): x, (0, 1, 0): y, (0, 0, 1): z}
    second = {
        (2, 0, 0): xx,
        (1, 1, 0): 2.0 * xy,
        (1, 0, 1): 2.0 * xz,
        (0, 2, 0): yy,
        (0, 1, 1): 2.0 * yz,
        (0, 0, 2): zz,
    }
    x3, y3, z3 = 3.0 * x, 3.0 * y, 3.0 * z
    third = {
        (3, 0, 0): xx * x,
        (2, 1, 0): xx * y3,
        (2, 0, 1): xx * z3,
        (1, 2, 0): yy * x3,
        (1, 1, 1): xy * (2.0 * z3),
        (1, 0, 2): zz * x3,
        (0, 3, 0): yy * y,
        (0, 2, 1): yy * z3,
        (0, 1, 2): zz * y3,
        (0, 0, 3): zz * z,
    }
    pairs = [t for t in TRIPLES if sum(t) == 2]
    trace2 = {t: column(42 + number) for number, t in enumerate(pairs)}
    grad = []
    q1, q2, q3, q4 = column(38), column(48), None, None
    for a in range(3):
        m1 = m[AXES[a]]
        a2 = contract(m, a, first)
        b2 = column(39 + a)
        a3 = contract(m, a, second)
        b3 = contract(trace2, a, first)
        a4 = contract(m, a, third)
        grad.append(
            m1 * u[1]
            + (a2 + (a2 - b2)) * u[2]
            + (a3 + 2.0 * (a3 - b3)) * u[3]
            + (4.0 * a4) * u[4]
        )
        q1 = q1 + r[a] * m1
        q2 = q2 + r[a] * (a2 - b2)
        low, high = r[a] * (a3 - b3), r[a] * a4
        q3 = low if q3 is None else q3 + low
        q4 = high if q4 is None else q4 + high
    pull = (
        m[(0, 0, 0)] * u[1] + 3.0 * q1 * u[2] + 5.0 * q2 * u[3] + 7.0 * q3 * u[4] + 9.0 * q4 * u[5]
    )
    return [grad[a] - r[a] * pull for a in range(3)]


def far_cells(sub, total, list_ref, pool_ref, out_ref, targets, order, picked):
    place = lax.broadcasted_iota(jnp.int32, (8, 128), 0)

    def visit(n, carry):
        row = order[n]
        listed = listed_row(sub, row)
        count = 0
        for k in range(16):
            entry = list_ref[k, listed]
            at = pl.ds(count, 1)
            picked[at, :] = pool_ref[(entry >> 4) * (EARLY + 1) + EARLY, pl.ds(entry & (RQC - 1), 1), :]
            count = count + jnp.where(((entry >> 3) & 1) == sub, 1, 0)
        half, b = row >> 5, row & 31
        sides = load_targets(targets, half, b)

        def add_cells(step, sums):
            table = picked[pl.ds(pl.multiple_of(step * 8, 8), 8), :]
            table = jnp.where(place < count - step * 8, table, 0.0)
            return tuple(s + p for s, p in zip(sums, cell_pull(table, sides)))

        zero = jnp.zeros((8, BUCKET), F32)
        sums = lax.fori_loop(0, (count + 7) >> 3, add_cells, (zero, zero, zero))
        add_rows(out_ref, half, b, sums)
        return carry

    lax.fori_loop(0, total, visit, 0)


def early_kernel(
    sub_ref, act_ref, pairs_ref, far_ref, pos_ref, other_ref, pool_ref, part_ref, out_ref,
    owned_ref, targets, order, sums, one, two, picked,
):
    sub = sub_ref[0]
    targets[0] = pos_ref[...]
    targets[1] = other_ref[...]
    out_ref[...] = part_ref[...]

    def gather_owned(step, total):
        for part in range(4):
            total = total + pool_ref[(step * 4 + part) * (EARLY + 1) + EARLY]
        return total

    chips = pool_ref.shape[0] // (EARLY + 1)
    owned_ref[...] = lax.fori_loop(0, chips // 4, gather_owned, jnp.zeros((8, 128), F32))
    total = list_active(sub, act_ref, order)
    far_cells(sub, total, far_ref, pool_ref, out_ref, targets, order, picked)
    near_pairs(0, total, pairs_ref, pool_ref, out_ref, (targets, order, sums, one, two))


def finish_kernel(sub_ref, act_ref, part_ref, came_ref, old_ref, owned_ref, accel_ref, parent_ref):
    sub = sub_ref[0]
    for b in range(NB):
        at = pl.ds(b * BUCKET, BUCKET)
        live = act_ref[sub * NB + b] > 0
        accel_ref[:, at] = jnp.where(live, part_ref[:, at] + came_ref[0:3, at], old_ref[:, at])
    for r in range(8):
        row = owned_ref[r : r + 1, :] + came_ref[3:4, 128 * r : 128 * r + 128]
        parent_ref[r : r + 1, :] = row[:, 0:35]
        parent_ref[8 + r : 9 + r, :] = row[:, 35:70]


def shape(*dims):
    return jax.ShapeDtypeStruct(dims, F32)


def local(
    positions,
    masses,
    old_accel,
    active,
    parent_of,
    parent_centers,
    local_list,
    near_list,
    far_list,
    send_ids,
    cell_send_ids,
):
    chips = lax.axis_size("dom")
    own = NB * BUCKET
    me = lax.axis_index("sub").astype(jnp.int32).reshape(1)
    swap = [(0, 1), (1, 0)]
    near_scratch = [
        pltpu.VMEM((2, 3, own), F32),
        pltpu.SMEM((2 * NB + 8,), jnp.int32),
        pltpu.VMEM((2 * NB + 1, 3, 8, BUCKET), F32),
        pltpu.VMEM((8, 128, 128), F32),
        pltpu.VMEM((8, 128, 128), F32),
    ]
    params = pltpu.CompilerParams(vmem_limit_bytes=32 << 20)

    other = lax.ppermute(positions, "sub", swap)

    tiles, first = pl.pallas_call(
        pack_kernel,
        in_specs=[SMEM, SMEM, SMEM, SMEM, VMEM, VMEM],
        out_specs=[VMEM, VMEM],
        out_shape=[shape(NB, 8, 128), shape(chips, EARLY + 1, 8, 128)],
        scratch_shapes=[
            pltpu.VMEM((4, NB, BUCKET), F32),
            pltpu.VMEM((3, NB, 128), F32),
            pltpu.VMEM((2, NB, 128), F32),
            pltpu.VMEM((NB, 128), F32),
            pltpu.VMEM((chips * 8, 128), F32),
        ],
        compiler_params=pltpu.CompilerParams(vmem_limit_bytes=60 << 20),
        name="pack",
    )(send_ids[0].T, cell_send_ids[0].T, parent_of, parent_centers, positions, masses.reshape(1, own))

    def exchange(blocks):
        flat = blocks.reshape(chips, -1, 128)
        came = lax.all_to_all(flat, "dom", split_axis=0, concat_axis=0, tiled=True)
        return came.reshape(blocks.shape)

    pool = exchange(first)

    part, pairs = pl.pallas_call(
        local_kernel,
        in_specs=[SMEM, SMEM, SMEM, SMEM, VMEM, VMEM, VMEM],
        out_specs=[VMEM, SMEM],
        out_shape=[shape(2, 3, own), jax.ShapeDtypeStruct((4 * SPAN + 16,), jnp.int32)],
        scratch_shapes=near_scratch
        + [pltpu.SMEM(((NB + 1) * USES,), jnp.int32), pltpu.SMEM((NB + 1,), jnp.int32)],
        compiler_params=params,
        cost_estimate=pl.CostEstimate(flops=2 << 30, transcendentals=1 << 27, bytes_accessed=1 << 20),
        name="near_local",
    )(me, active, local_list.T, near_list.T, positions, other, tiles)

    second = pl.pallas_call(
        pack_late_kernel,
        in_specs=[SMEM, VMEM],
        out_specs=VMEM,
        out_shape=shape(chips, RQ - EARLY, 8, 128),
        compiler_params=params,
        cost_estimate=pl.CostEstimate(flops=1 << 20, transcendentals=0, bytes_accessed=2 << 20),
        name="pack_late",
    )(send_ids[0].T, tiles)
    pool, second, part = lax.optimization_barrier((pool, second, part))
    late_pool = exchange(second)

    part, owned = pl.pallas_call(
        early_kernel,
        in_specs=[SMEM, SMEM, SMEM, SMEM, VMEM, VMEM, VMEM, VMEM],
        out_specs=[VMEM, VMEM],
        out_shape=[shape(2, 3, own), shape(8, 128)],
        scratch_shapes=near_scratch + [pltpu.VMEM((24, 128), F32)],
        compiler_params=params,
        cost_estimate=pl.CostEstimate(flops=2 << 30, transcendentals=1 << 27, bytes_accessed=1 << 20),
        name="early",
    )(me, active, pairs, far_list.T, positions, other, pool.reshape(-1, 8, 128), part)
    part, send = pl.pallas_call(
        late_kernel,
        in_specs=[SMEM, SMEM, SMEM, VMEM, VMEM, VMEM, VMEM, VMEM],
        out_specs=[VMEM, VMEM],
        out_shape=[shape(3, own), shape(4, own)],
        scratch_shapes=near_scratch + [pltpu.VMEM((2, 3, own), F32)],
        compiler_params=params,
        cost_estimate=pl.CostEstimate(flops=1 << 30, transcendentals=1 << 26, bytes_accessed=1 << 20),
        name="late",
    )(me, active, pairs, positions, other, late_pool.reshape(-1, 8, 128), part, owned)

    came = lax.ppermute(send, "sub", swap)
    accel, parents = pl.pallas_call(
        finish_kernel,
        in_specs=[SMEM, SMEM, VMEM, VMEM, VMEM, VMEM],
        out_specs=[VMEM, VMEM],
        out_shape=[shape(3, own), shape(16, 35)],
        compiler_params=params,
        name="finish",
    )(me, active, part, came, old_accel, owned)
    return accel, parents.T


def solution(mesh):
    both = ("dom", "sub")
    in_specs = (
        P(None, both),
        P(both),
        P(None, both),
        P("dom"),
        P(both),
        P(),
        P("dom", None),
        P("dom", None),
        P("dom", None),
        P(both, None, None),
        P(both, None, None),
    )
    out_specs = (P(None, both), P(None, "dom"))
    return jax.shard_map(local, mesh=mesh, in_specs=in_specs, out_specs=out_specs, check_vma=False)
```
